512 devices in a mesh: dp: 128 (over y, z, core), tensor: 4 (over x).
Axes of the slice: x: 4, y: 4, z: 16, core: 2. Of those that a mesh axis runs over, the one named last changes fastest.
Arguments:
- face_grads: bfloat16 [32768, 2048], P('dp', 'tensor'), may hold values from -6 to 6
- face_owner: int32 [32768, 1], P('dp'), may hold values from 0 to 127; in each aligned block of 256 rows (0 to 255, 256 to 511, ...) at most 4 rows name the same one
- face_slot: int32 [32768, 1], P('dp'), may hold values from 0 to 255
- queries: bfloat16 [32768, 1024], P('dp', 'tensor'), may hold values from -6 to 6
- context_keys: bfloat16 [512, 1024], P(None, 'tensor'), may hold values from -6 to 6
- context_values: bfloat16 [512, 1024], P(None, 'tensor'), may hold values from -6 to 6
- w_out: bfloat16 [1024, 2048], P('tensor'), may hold values from -0.1875 to 0.1875
- branch_gate: float32 [2048], replicated, may hold values from 0.3 to 3
Outputs:
- grad_q: bfloat16 [32768, 1024], P('dp', 'tensor')
- grad_wo_t: float32 [2048, 1024], P('dp', 'tensor')
- grad_k: float32 [512, 1024], P('dp', 'tensor')
- grad_v: float32 [512, 1024], P('dp', 'tensor')
The draws below stay inside these ranges and needn't reach their ends.
Inputs may be any that keep to these rules, and one draw needn't show every extreme that they name: `face_owner`: at most 4 of the 256 face rows of one dp index name the same owner.
All inputs are finite; a program needn't handle non-finite values.
Results may differ from the reference program's by a relative error of at most 0.03.
Values may be sent and summed in bfloat16 or wider, within the bound.
A program may use at most 64 MiB of HBM per device.

```python
import math
import jax
import jax.numpy as jnp
import numpy as np
from jax import lax

D = 2048
HEADS = 8
HD = 128
CTX = 512
TOK_DEV = 256
FACE_DEV = 256
CAP = 4
TOKENS = 32768
FACES = 32768
N_DP = 128


def draw_context_keys(key, part):
    normal_part = jnp.clip(jax.random.normal(jax.random.fold_in(key, 3), (CTX, HEADS, HD), jnp.float32), -6.0, 6.0)
    return normal_part.reshape(CTX, HEADS * HD).astype(jnp.bfloat16)


def draw_queries(key, part):
    normal_part = jnp.clip(jax.random.normal(jax.random.fold_in(key, 5), (TOKENS, HEADS, HD), jnp.float32), -6.0, 6.0)
    return normal_part.reshape(TOKENS, HEADS * HD).astype(jnp.bfloat16)


def touch_ends(values, own_key, low, top_value):
    spot = [jax.random.randint(jax.random.fold_in(own_key, axis), (), 0, length) for axis, length in enumerate(values.shape)]
    longest = values.shape.index(max(values.shape))
    beside = spot[:longest] + [(spot[longest] + 1) % values.shape[longest]] + spot[longest + 1:]
    return values.at[tuple(spot)].set(low).at[tuple(beside)].set(top_value)


def shard_levels(key, shape, pieces, smallest, top_value):
    def one(position, shards_of):
        heights = jax.random.uniform(jax.random.fold_in(jax.random.fold_in(key, 6), position), (shards_of,), jnp.float32, smallest / len(pieces), top_value / len(pieces))
        return jnp.repeat(jnp.exp(heights), shape[position] // shards_of).reshape((-1,) + (1,) * (len(shape) - position - 1))

    level = one(*pieces[0])
    for cut in pieces[1:]:
        level = level * one(*cut)
    return level


def routed_block(key, own, number, rows, count, top, most, slope):
    ranking = jax.random.permutation(key, count)
    heavy_load, usual = load_shares(count, rows * top, most, slope, True), load_shares(count, rows * top, most, slope, False)
    places = jnp.arange(count)

    def named(sizes, turn):
        used = int((sizes > 0).sum())
        fixed = max(1, used // 4)
        shifted = fixed + (places - fixed + turn * (used - fixed)) % max(1, count - fixed)
        return jnp.zeros((count,), jnp.int32).at[ranking[jnp.where(places < fixed, places, shifted)]].set(jnp.asarray(sizes, jnp.int32))

    sizes = jnp.where(number % 4 == 0, named(heavy_load, number // 4), named(usual, number - number // 4 - 1))
    mixed = jax.random.permutation(jax.random.fold_in(own, 3), count)
    giver, taker = mixed[0:count // 2 * 2:2], mixed[1:count // 2 * 2:2]
    margin = jnp.minimum(sizes[giver] - 1, most - sizes[taker]) // 2
    margin = jnp.where((giver == ranking[0]) | (taker == ranking[0]) | (sizes[taker] == 0), 0, jnp.maximum(margin, 0))
    shifted = jax.random.randint(jax.random.fold_in(own, 4), (count // 2,), 0, 1 << 20) % (margin + 1)
    sizes = sizes.at[giver].add(-shifted).at[taker].add(shifted)
    items = jnp.searchsorted(jnp.cumsum(sizes), jnp.arange(rows * top), side="right").astype(jnp.int32)
    table = items.reshape(top, rows).T
    table = table[jax.random.permutation(jax.random.fold_in(own, 1), rows)]
    turn = jax.random.randint(jax.random.fold_in(own, 2), (rows, 1), 0, top)
    return jnp.take_along_axis(table, (jnp.arange(top)[None, :] + turn) % top, axis=1)


def load_shares(number_of, total, most, slope, full):
    portions = [(1 << 20) // math.isqrt(grade ** slope) + 1 for grade in range(1, number_of + 1)]
    largest = most if full else min(most, max(-(-total // number_of), total * portions[0] // sum(portions)))
    least = 1 if total - largest >= number_of - 1 else 0
    given, rest = [largest] + [least] * (number_of - 1), total - largest - least * (number_of - 1)
    while rest > 0:
        candidates = [i for i in range(1, number_of) if given[i] < largest] or [i for i in range(1, number_of) if given[i] < most]
        mass, left = sum([portions[i] for i in candidates]), rest
        for i in candidates:
            extra = min(most - given[i], max(1, left * portions[i] // mass), rest)
            given[i] = given[i] + extra
            rest = rest - extra
    return np.array(given)


def bell_draw(own_key, extent, width, most, shards=(), kind=jnp.bfloat16):
    factor_of = shard_levels(own_key, extent, shards, -0.22, 0.18) if shards else 1.0
    result = jax.random.normal(own_key, extent, jnp.float32) * width * factor_of
    return jnp.minimum(jnp.maximum(result, -most), most).astype(kind)


def setup_inputs(seed: int = 0) -> dict:
    arg_keys = jax.random.split(jax.random.key(seed), 9)
    face_grads = bell_draw(arg_keys[0], (FACES, D), 1.0, 6.0, ((0, 128), (1, 4)))
    face_owner_keys = jax.random.split(jax.random.fold_in(arg_keys[1], 1), FACES // FACE_DEV)
    face_owner_turns = jax.random.permutation(jax.random.fold_in(arg_keys[1], 3), FACES // FACE_DEV)
    face_owner = jax.vmap(lambda own, number: routed_block(jax.random.fold_in(arg_keys[1], 2), own, number, FACE_DEV, N_DP, 1, CAP, 2))(face_owner_keys, face_owner_turns).reshape((FACES, 1))
    face_slot = touch_ends(jax.random.randint(arg_keys[2], (FACES, 1), 0, TOK_DEV), jax.random.fold_in(arg_keys[2], 1), 0, TOK_DEV - 1).astype(jnp.int32)
    queries = draw_queries(jax.random.fold_in(arg_keys[8], 71), 0)
    context_keys = draw_context_keys(jax.random.fold_in(arg_keys[8], 71), 0)
    context_values = bell_draw(arg_keys[5], (CTX, HEADS * HD), 1.0, 6.0, ((1, 4),))
    w_out = bell_draw(arg_keys[6], (HEADS * HD, D), (HEADS * HD) ** -0.5, 0.1875, ((0, 4),))
    branch_gate = jnp.clip(jnp.exp(jax.random.uniform(arg_keys[7], (D,), jnp.float32, math.log(0.3), math.log(3.0))), 0.3, 3.0)
    return dict(face_grads=face_grads, face_owner=face_owner, face_slot=face_slot, queries=queries, context_keys=context_keys, context_values=context_values, w_out=w_out, branch_gate=branch_gate)


def reference(face_grads, face_owner, face_slot, queries, context_keys, context_values, w_out, branch_gate):
    token_index = (face_owner[:, 0] * TOK_DEV + face_slot[:, 0]).astype(jnp.int32)
    grad_out = jax.ops.segment_sum(face_grads.astype(jnp.float32), token_index, num_segments=TOKENS).astype(jnp.bfloat16)
    branch_grad = (branch_gate[None, :] * grad_out.astype(jnp.float32)).astype(jnp.bfloat16)
    grad_attn = jnp.dot(branch_grad, w_out.T, preferred_element_type=jnp.float32).astype(jnp.bfloat16)
    score_scale = 1.0 / math.sqrt(HD)
    keys_f = context_keys.astype(jnp.float32).reshape(CTX, HEADS, HD)
    values_f = context_values.astype(jnp.float32).reshape(CTX, HEADS, HD)
    block_rows = math.gcd(TOKENS, 4096)
    block_total = TOKENS // block_rows

    def block_step(totals, block_index):
        first_row = (block_index * block_rows).astype(jnp.int32)
        query_block = lax.dynamic_slice_in_dim(queries, first_row, block_rows, 0).astype(jnp.float32).reshape(block_rows, HEADS, HD)
        attn_grad_bf = lax.dynamic_slice_in_dim(grad_attn, first_row, block_rows, 0)
        attn_grad = attn_grad_bf.astype(jnp.float32).reshape(block_rows, HEADS, HD)
        branch_block = lax.dynamic_slice_in_dim(branch_grad, first_row, block_rows, 0)
        scores = jnp.einsum('thd,chd->htc', query_block, keys_f) * score_scale
        weights = jax.nn.softmax(scores, axis=-1)
        probs_bf = lax.optimization_barrier(weights.astype(jnp.bfloat16))
        probs_f = probs_bf.astype(jnp.float32)
        attention = jnp.einsum('htc,chd->thd', probs_f, values_f).astype(jnp.bfloat16).reshape(block_rows, HEADS * HD)
        wo_term = jnp.dot(branch_block.T, attention, preferred_element_type=jnp.float32)
        grad_probs = jnp.einsum('thd,chd->htc', attn_grad, values_f)
        row_delta = lax.optimization_barrier(jnp.sum(weights * grad_probs, axis=-1, keepdims=True))
        score_bf = lax.optimization_barrier((weights * (grad_probs - row_delta)).astype(jnp.bfloat16))
        score_grad = score_bf.astype(jnp.float32)
        query_grad = (score_scale * jnp.einsum('htc,chd->thd', score_grad, keys_f)).astype(jnp.bfloat16).reshape(block_rows, HEADS * HD)
        key_term = score_scale * jnp.einsum('htc,thd->chd', score_grad, query_block)
        value_term = jnp.einsum('htc,thd->chd', probs_f, attn_grad)
        new_totals = (totals[0] + wo_term, totals[1] + key_term.reshape(CTX, HEADS * HD), totals[2] + value_term.reshape(CTX, HEADS * HD))
        return (new_totals, query_grad)
    start_totals = (jnp.zeros((D, HEADS * HD), jnp.float32), jnp.zeros((CTX, HEADS * HD), jnp.float32), jnp.zeros((CTX, HEADS * HD), jnp.float32))
    totals, query_blocks = lax.scan(block_step, start_totals, jnp.arange(block_total, dtype=jnp.int32))
    grad_q = query_blocks.reshape(TOKENS, HEADS * HD)
    return (grad_q, totals[0], totals[1], totals[2])
```

```python
import functools
import math

import jax
import jax.numpy as jnp
from jax import lax
from jax.experimental import pallas as pl
from jax.experimental.pallas import tpu as pltpu
from jax.sharding import PartitionSpec as P

HD = 128
LANES = 128
CORES = 2
MESH = pl.DeviceIdType.MESH
F32 = jnp.float32
BF16 = jnp.bfloat16


def iota(shape, axis):
    return lax.broadcasted_iota(jnp.int32, shape, axis)


def log2(n):
    bits = n.bit_length() - 1
    assert 1 << bits == n
    return bits


def one_hot(cond):
    return jnp.where(cond, 1.0, 0.0).astype(BF16)


def dot(a, b, dims=((1,), (0,))):
    return lax.dot_general(a, b, (dims, ((), ())), preferred_element_type=F32)


NT = ((1,), (1,))
TN = ((0,), (0,))


def kernel(
    nx,
    nz,
    face_ref,
    owner_ref,
    slot_ref,
    q_ref,
    k_ref,
    v_ref,
    w_ref,
    gate_ref,
    gq_ref,
    gwo_ref,
    gk_ref,
    gv_ref,
    out_a,
    in_a,
    mout_a,
    min_a,
    m2d,
    min_b,
    out_b,
    in_b,
    wall,
    aall,
    ga_out,
    ga_in,
    wo_out,
    wo_in,
    wz_out,
    wz_in,
    kv_out,
    kv_in,
    kz_out,
    kz_in,
    wts,
    probs,
    kp,
    vp,
    bg,
    perm_b,
    send,
    recv_a,
    recv_b,
    recv,
):
    ny = nx
    np_ = ny * CORES
    ch, _, ma, _ = out_a.shape
    faces, dx = face_ref.shape
    tok, hw = q_ref.shape
    ctx = k_ref.shape[0]
    heads = hw // HD
    places = nz * ma
    cap = ma // np_
    rw = gwo_ref.shape[0]
    kr = gk_ref.shape[0]
    halves = hw // LANES
    lanes_m = m2d.shape[1]
    scale = 1.0 / math.sqrt(HD)

    d = lax.axis_index("dp")
    x = lax.axis_index("tensor")
    c = lax.rem(d, CORES)
    z = lax.rem(lax.div(d, CORES), nz)
    y = lax.div(d, CORES * nz)
    p = y * CORES + c

    def z_peer(k):
        zz = lax.rem(z + k, nz)
        return zz, (y * nz + zz) * CORES + c

    def p_peer(k):
        pp = lax.rem(p + k, np_)
        return pp, (lax.div(pp, CORES) * nz + z) * CORES + lax.rem(pp, CORES)

    def t_peer(k):
        zz = lax.rem(z + k, nz)
        return zz, (x * nz + zz) * CORES + c

    def loop(lo, hi, f):
        def step(i, carry):
            f(i)
            return carry

        lax.fori_loop(lo, hi, step, 0)

    def push(src, dst, ssem, rsem, dev):
        pltpu.make_async_remote_copy(
            src_ref=src, dst_ref=dst, send_sem=ssem, recv_sem=rsem, device_id=dev, device_id_type=MESH
        ).start()

    def wait_recv(view, rsem):
        pltpu.make_async_remote_copy(
            src_ref=view, dst_ref=view, send_sem=send.at[0], recv_sem=rsem, device_id=(d, x), device_id_type=MESH
        ).wait_recv()

    def wait_send(view, ssem):
        pltpu.make_async_remote_copy(
            src_ref=view, dst_ref=view, send_sem=ssem, recv_sem=recv.at[0], device_id=(d, x), device_id_type=MESH
        ).wait_send()

    barrier = pltpu.get_barrier_semaphore()

    def greet(dev):
        pl.semaphore_signal(barrier, inc=1, device_id=dev, device_id_type=MESH)

    loop(1, nz, lambda k: greet((z_peer(k)[1], x)))
    loop(1, np_, lambda k: greet((p_peer(k)[1], x)))
    loop(1, nx, lambda k: greet((d, lax.rem(x + k, nx))))

    @pl.when(x != y)
    def _():
        loop(0, nz, lambda k: greet((t_peer(k)[1], y)))

    owner = owner_ref[...]
    owner_f = owner.astype(F32)
    sub, lane = iota((faces, faces), 0), iota((faces, faces), 1)
    owner_col = jnp.sum(jnp.where(sub == lane, owner_f, 0.0), axis=1, keepdims=True)
    rank = jnp.sum(
        jnp.where((owner_col == owner_f) & (sub < lane), 1.0, 0.0), axis=0, keepdims=True
    ).astype(jnp.int32)
    oc = owner & (CORES - 1)
    oz = (owner >> log2(CORES)) & (nz - 1)
    oy = owner >> log2(CORES * nz)
    place = ((oz * ny + oy) * CORES + oc) * cap + rank
    placed = iota((places, faces), 0) == place
    slot_col = (
        jnp.sum(jnp.where(placed, slot_ref[...].astype(F32) + 1.0, 0.0), axis=1, keepdims=True) - 1.0
    )
    spread = jnp.where(
        iota((places, lanes_m), 1) == (iota((places, lanes_m), 0) & (ma - 1)), slot_col, 0.0
    ).astype(BF16)
    by_z = one_hot(iota((nz, places), 0) == (iota((nz, places), 1) >> log2(ma)))
    meta = dot(by_z, spread)
    for i in range(nz):
        mout_a[i] = meta[i : i + 1, :]
    min_a[z] = mout_a[z]
    place_hot = one_hot(placed)

    def fill(i):
        part = dot(place_hot, face_ref[:, i * LANES : (i + 1) * LANES]).astype(BF16)
        out_a[i] = part.reshape(nz, ma, LANES)
        in_a[i, z] = out_a[i, z]

    fill(0)
    pl.semaphore_wait(barrier, (nz - 1) + (np_ - 1) + (nx - 1) + jnp.where(x == y, 0, nz))

    def send_meta(k):
        zz, dev = z_peer(k)
        push(mout_a.at[zz], min_a.at[z], send.at[0], recv.at[0], (dev, x))

    loop(1, nz, send_meta)

    def send_a(i):
        def step(k):
            zz, dev = z_peer(k)
            push(out_a.at[i, zz], in_a.at[i, z], send.at[1], recv_a.at[i], (dev, x))

        loop(1, nz, step)

    send_a(0)

    def send_w(k):
        xx = lax.rem(x + k, nx)
        push(
            w_ref.at[:, pl.ds(pl.multiple_of(xx * dx, LANES), dx)],
            wall.at[x],
            send.at[2],
            recv.at[1],
            (d, xx),
        )

    loop(1, nx, send_w)
    for i in range(1, ch):
        fill(i)
        send_a(i)
    wall[x] = w_ref[:, pl.ds(pl.multiple_of(x * dx, LANES), dx)]

    new, old = iota((ctx, ctx), 0), iota((ctx, ctx), 1)
    b_k, b_z, b_c = log2(kr), log2(nz), log2(CORES)
    o_k = old & (kr - 1)
    o_c = (old >> b_k) & (CORES - 1)
    o_z = (old >> (b_k + b_c)) & (nz - 1)
    o_y = old >> (b_k + b_c + b_z)
    perm_k = one_hot(new == ((o_y * CORES + o_c) * nz + o_z) * kr + o_k)
    kp[...] = dot(perm_k, k_ref[...]).astype(BF16)
    vp[...] = dot(perm_k, v_ref[...]).astype(BF16)
    for h in range(heads):
        cols = slice(h * HD, (h + 1) * HD)
        scores = dot(q_ref[:, cols], kp[:, cols], NT) * scale
        top = jnp.max(scores, axis=-1, keepdims=True)
        e = jnp.exp(scores - top)
        w = e / jnp.sum(e, axis=-1, keepdims=True)
        wts[h] = w
        pb = w.astype(BF16)
        probs[h] = pb
        aall[x, :, cols] = dot(pb, vp[:, cols]).astype(BF16)

    def send_att(k):
        xx = lax.rem(x + k, nx)
        push(aall.at[x], aall.at[x], send.at[3], recv.at[2], (d, xx))

    loop(1, nx, send_att)

    new, old = iota((places, places), 0), iota((places, places), 1)
    o_r = old & (cap - 1)
    o_p = (old >> log2(cap)) & (np_ - 1)
    o_z = old >> log2(ma)
    perm_b[...] = one_hot(new == (o_p * nz + o_z) * cap + o_r)

    wait_recv(min_a.at[pl.ds(0, nz - 1)], recv.at[0])
    for i in range(nz):
        m2d[i : i + 1, :] = min_a[i]
    min_b[p] = m2d[...]

    def send_mb(k):
        _, dev = p_peer(k)
        push(m2d, min_b.at[p], send.at[4], recv.at[3], (dev, x))

    loop(1, np_, send_mb)

    for i in range(ch):
        wait_recv(in_a.at[i, pl.ds(0, nz - 1)], recv_a.at[i])
        moved = dot(perm_b[...], in_a[i].reshape(places, LANES)).astype(BF16)
        out_b[i] = moved.reshape(np_, nz * cap, LANES)
        in_b[i, p] = out_b[i, p]

        def send_b(k, i=i):
            pp, dev = p_peer(k)
            push(out_b.at[i, pp], in_b.at[i, p], send.at[5], recv_b.at[i], (dev, x))

        loop(1, np_, send_b)

    wait_recv(min_b.at[pl.ds(0, np_ - 1)], recv.at[3])
    pick = one_hot(
        iota((lanes_m, places), 0) == p * cap + (iota((lanes_m, places), 1) & (cap - 1))
    )
    table = dot(min_b[...].reshape(np_ * nz, lanes_m).astype(BF16), pick)
    slot_row = jnp.sum(
        jnp.where(
            iota((np_ * nz, places), 0) == (iota((np_ * nz, places), 1) >> log2(cap)), table, 0.0
        ),
        axis=0,
        keepdims=True,
    )
    land = one_hot(iota((tok, places), 0).astype(F32) == slot_row)
    gate = gate_ref[:, pl.ds(pl.multiple_of(x * dx, LANES), dx)]
    for i in range(ch):
        cols = slice(i * LANES, (i + 1) * LANES)
        wait_recv(in_b.at[i, pl.ds(0, np_ - 1)], recv_b.at[i])
        grad_out = dot(land, in_b[i].reshape(places, LANES)).astype(BF16)
        bg[:, cols] = (gate[:, cols] * grad_out.astype(F32)).astype(BF16)

    wait_recv(wall.at[pl.ds(0, nx - 1)], recv.at[1])

    def project(k):
        xx = lax.rem(x + k, nx)
        ga_out[xx] = dot(bg[...], wall[xx], NT).astype(BF16)
        push(ga_out.at[xx], ga_in.at[x], send.at[6], recv.at[4], (d, xx))

    loop(1, nx, project)
    ga_in[x] = dot(bg[...], wall[x], NT).astype(BF16)

    wait_recv(aall.at[pl.ds(0, nx - 1)], recv.at[2])

    def outer(xx):
        part = dot(bg[...], aall[xx], TN).astype(BF16).reshape(nz, CORES, rw, hw)
        for cc in range(CORES):
            wo_out[xx * CORES + cc] = part[:, cc]

    loop(0, ny, outer)
    wo_in[p] = wo_out[p]

    def send_wo(k):
        pp, dev = p_peer(k)
        push(wo_out.at[pp], wo_in.at[p], send.at[7], recv.at[5], (dev, x))

    loop(1, np_, send_wo)

    wait_recv(ga_in.at[pl.ds(0, nx - 1)], recv.at[4])
    total = ga_in[0].astype(F32)
    for i in range(1, nx):
        total = total + ga_in[i].astype(F32)
    ga = total.astype(BF16)
    for h in range(heads):
        cols = slice(h * HD, (h + 1) * HD)
        ga_h = ga[:, cols]
        gp = dot(ga_h, vp[:, cols], NT)
        w = wts[h]
        delta = jnp.sum(w * gp, axis=-1, keepdims=True)
        sg = (w * (gp - delta)).astype(BF16)
        gk_h = (scale * dot(sg, q_ref[:, cols], TN)).astype(BF16)
        gv_h = dot(probs[h], ga_h, TN).astype(BF16)
        kv_out[:, 0, :, cols] = gk_h.reshape(np_, nz * kr, HD)
        kv_out[:, 1, :, cols] = gv_h.reshape(np_, nz * kr, HD)
        gq_ref[:, cols] = (scale * dot(sg, kp[:, cols])).astype(BF16)
    kv_in[p] = kv_out[p]

    def send_kv(k):
        pp, dev = p_peer(k)
        push(kv_out.at[pp], kv_in.at[p], send.at[8], recv.at[6], (dev, x))

    loop(1, np_, send_kv)

    wait_recv(wo_in.at[pl.ds(0, np_ - 1)], recv.at[5])

    def sum_wo(i):
        acc = wo_in[0, i].astype(F32)
        for j in range(1, np_):
            acc = acc + wo_in[j, i].astype(F32)
        wz_out[i] = acc.astype(BF16)

    loop(0, nz, sum_wo)

    def send_wz(k):
        zz, dev = t_peer(k)
        push(wz_out.at[zz], wz_in.at[z], send.at[9], recv.at[7], (dev, y))

    @pl.when(x != y)
    def _():
        send_wz(0)

    @pl.when(x == y)
    def _():
        wz_in[z] = wz_out[z]

    loop(1, nz, send_wz)

    wait_recv(kv_in.at[pl.ds(0, np_ - 1)], recv.at[6])
    rows = 2 * halves * kr
    acc = None
    for j in range(2):
        tot = kv_in[0, j].astype(F32)
        for i in range(1, np_):
            tot = tot + kv_in[i, j].astype(F32)
        tot = tot.astype(BF16)
        for h in range(halves):
            r, s = iota((nz * rows, nz * kr), 0), iota((nz * rows, nz * kr), 1)
            inner = r & (rows - 1)
            sel = (
                ((r >> log2(rows)) == (s >> b_k))
                & ((inner >> b_k) == j * halves + h)
                & ((inner & (kr - 1)) == (s & (kr - 1)))
            )
            part = dot(one_hot(sel), tot[:, h * LANES : (h + 1) * LANES])
            acc = part if acc is None else acc + part
    kz_out[...] = acc.astype(BF16).reshape(nz, rows, LANES)
    kz_in[z] = kz_out[z]

    def send_kz(k):
        zz, dev = z_peer(k)
        push(kz_out.at[zz], kz_in.at[z], send.at[10], recv.at[8], (dev, x))

    loop(1, nz, send_kz)

    @pl.when(x != y)
    def _():
        wait_recv(wz_in, recv.at[7])

    @pl.when(x == y)
    def _():
        wait_recv(wz_in.at[pl.ds(0, nz - 1)], recv.at[7])

    acc = wz_in[0].astype(F32)
    for i in range(1, nz):
        acc = acc + wz_in[i].astype(F32)
    gwo_ref[...] = acc

    wait_recv(kz_in.at[pl.ds(0, nz - 1)], recv.at[8])
    acc = kz_in[0].astype(F32)
    for i in range(1, nz):
        acc = acc + kz_in[i].astype(F32)
    for h in range(halves):
        cols = slice(h * LANES, (h + 1) * LANES)
        gk_ref[:, cols] = acc[h * kr : (h + 1) * kr, :]
        gv_ref[:, cols] = acc[(halves + h) * kr : (halves + h + 1) * kr, :]

    wait_send(mout_a.at[pl.ds(0, nz - 1)], send.at[0])
    wait_send(out_a.at[:, pl.ds(0, nz - 1)], send.at[1])
    wait_send(wall.at[pl.ds(0, nx - 1)], send.at[2])
    wait_send(aall.at[pl.ds(0, nx - 1)], send.at[3])
    wait_send(min_b.at[pl.ds(0, np_ - 1)], send.at[4])
    wait_send(out_b.at[:, pl.ds(0, np_ - 1)], send.at[5])
    wait_send(ga_out.at[pl.ds(0, nx - 1)], send.at[6])
    wait_send(wo_out.at[pl.ds(0, np_ - 1)], send.at[7])
    wait_send(kv_out.at[pl.ds(0, np_ - 1)], send.at[8])

    @pl.when(x != y)
    def _():
        wait_send(wz_out, send.at[9])

    @pl.when(x == y)
    def _():
        wait_send(wz_out.at[pl.ds(0, nz - 1)], send.at[9])

    wait_send(kz_out.at[pl.ds(0, nz - 1)], send.at[10])


def body(face_grads, face_owner, face_slot, queries, keys, values, w_out, branch_gate):
    nx = lax.axis_size("tensor")
    dp = lax.axis_size("dp")
    ny = nx
    nz = dp // (ny * CORES)
    np_ = ny * CORES
    faces, dx = face_grads.shape
    tok, hw = queries.shape
    ctx = keys.shape[0]
    heads = hw // HD
    cap = 2 * faces // dp
    ch = dx // LANES
    ma = np_ * cap
    places = nz * ma
    width = w_out.shape[1]
    rw = width // dp
    kr = ctx // dp
    rows = 2 * (hw // LANES) * kr
    lanes_m = max(LANES, ma)
    vmem = pltpu.VMEM
    dma = pltpu.SemaphoreType.DMA
    spec = pl.BlockSpec(memory_space=pltpu.VMEM)
    return pl.pallas_call(
        functools.partial(kernel, nx, nz),
        out_shape=(
            jax.ShapeDtypeStruct((tok, hw), BF16),
            jax.ShapeDtypeStruct((rw, hw), F32),
            jax.ShapeDtypeStruct((kr, hw), F32),
            jax.ShapeDtypeStruct((kr, hw), F32),
        ),
        in_specs=[spec] * 8,
        out_specs=(spec,) * 4,
        scratch_shapes=[
            vmem((ch, nz, ma, LANES), BF16),
            vmem((ch, nz, ma, LANES), BF16),
            vmem((nz, 1, lanes_m), F32),
            vmem((nz, 1, lanes_m), F32),
            vmem((nz, lanes_m), F32),
            vmem((np_, nz, lanes_m), F32),
            vmem((ch, np_, nz * cap, LANES), BF16),
            vmem((ch, np_, nz * cap, LANES), BF16),
            vmem((nx, hw, dx), BF16),
            vmem((nx, tok, hw), BF16),
            vmem((nx, tok, hw), BF16),
            vmem((nx, tok, hw), BF16),
            vmem((np_, nz, rw, hw), BF16),
            vmem((np_, nz, rw, hw), BF16),
            vmem((nz, rw, hw), BF16),
            vmem((nz, rw, hw), BF16),
            vmem((np_, 2, nz * kr, hw), BF16),
            vmem((np_, 2, nz * kr, hw), BF16),
            vmem((nz, rows, LANES), BF16),
            vmem((nz, rows, LANES), BF16),
            vmem((heads, tok, ctx), F32),
            vmem((heads, tok, ctx), BF16),
            vmem((ctx, hw), BF16),
            vmem((ctx, hw), BF16),
            vmem((tok, dx), BF16),
            vmem((places, places), BF16),
            dma((11,)),
            dma((ch,)),
            dma((ch,)),
            dma((9,)),
        ],
        compiler_params=pltpu.CompilerParams(
            collective_id=0, has_side_effects=True, vmem_limit_bytes=44 << 20
        ),
    )(
        face_grads,
        face_owner.reshape(1, faces),
        face_slot.reshape(1, faces),
        queries,
        keys,
        values,
        w_out,
        branch_gate.reshape(1, width),
    )


def solution(mesh):
    in_specs = (
        P("dp", "tensor"),
        P("dp", None),
        P("dp", None),
        P("dp", "tensor"),
        P(None, "tensor"),
        P(None, "tensor"),
        P("tensor", None),
        P(),
    )
    out_specs = (P("dp", "tensor"), P("dp", "tensor"), P("dp", "tensor"), P("dp", "tensor"))
    return jax.shard_map(body, mesh=mesh, in_specs=in_specs, out_specs=out_specs, check_vma=False)
```

```python
import functools
import math

import jax
import jax.numpy as jnp
from jax import lax
from jax.experimental import pallas as pl
from jax.experimental.pallas import tpu as pltpu
from jax.sharding import PartitionSpec as P

HD = 128
LANES = 128
CORES = 2
MESH = pl.DeviceIdType.MESH
F32 = jnp.float32
BF16 = jnp.bfloat16


def iota(shape, axis):
    return lax.broadcasted_iota(jnp.int32, shape, axis)


def log2(n):
    bits = n.bit_length() - 1
    assert 1 << bits == n
    return bits


def one_hot(cond):
    return jnp.where(cond, 1.0, 0.0).astype(BF16)


def dot(a, b, dims=((1,), (0,))):
    return lax.dot_general(a, b, (dims, ((), ())), preferred_element_type=F32)


NT = ((1,), (1,))
TN = ((0,), (0,))


def kernel(
    nx,
    nz,
    face_hbm,
    owner_hbm,
    slot_hbm,
    q_hbm,
    k_hbm,
    v_hbm,
    w_hbm,
    gate_hbm,
    gq_ref,
    gwo_ref,
    gk_ref,
    gv_ref,
    out_a,
    in_a,
    mout_a,
    min_a,
    m2d,
    min_b,
    out_b,
    in_b,
    aall,
    asib,
    bgx,
    bgt,
    bgt_in,
    wo_out,
    wo_in,
    wz_out,
    wz_in,
    kc_out,
    kc_in,
    ky_out,
    ky_in,
    kz_out,
    kz_in,
    wts,
    probs,
    kp,
    vp,
    ga_acc,
    perm_b,
    perm_w,
    w_ref,
    face_ref,
    owner_ref,
    slot_ref,
    q_ref,
    k_ref,
    v_ref,
    gate_ref,
    load,
    send,
    recv_a,
    recv_b,
    recv_x,
    recv,
):
    loads = [
        pltpu.make_async_copy(src, dst, load.at[i])
        for i, (src, dst) in enumerate(
            (
                (owner_hbm, owner_ref),
                (slot_hbm, slot_ref),
                (face_hbm, face_ref),
                (k_hbm, k_ref),
                (v_hbm, v_ref),
                (q_hbm, q_ref),
                (gate_hbm, gate_ref),
                (w_hbm, w_ref),
            )
        )
    ]
    for copy in loads:
        copy.start()

    ny = nx
    np_ = ny * CORES
    ch, _, ma, _ = out_a.shape
    faces, dx = face_ref.shape
    tok, hw = q_ref.shape
    ctx = k_ref.shape[0]
    heads = hw // HD
    places = nz * ma
    cap = ma // np_
    rw = gwo_ref.shape[0]
    kr = gk_ref.shape[0]
    halves = hw // LANES
    lanes_m = m2d.shape[1]
    scale = 1.0 / math.sqrt(HD)

    d = lax.axis_index("dp")
    x = lax.axis_index("tensor")
    c = lax.rem(d, CORES)
    z = lax.rem(lax.div(d, CORES), nz)
    y = lax.div(d, CORES * nz)
    p = y * CORES + c
    twin = d + 1 - 2 * c

    def z_peer(k):
        zz = lax.rem(z + k, nz)
        return zz, (y * nz + zz) * CORES + c

    def p_peer(k):
        pp = lax.rem(p + k, np_)
        return pp, (lax.div(pp, CORES) * nz + z) * CORES + lax.rem(pp, CORES)

    def y_peer(k):
        yy = lax.rem(y + k, ny)
        return yy, (yy * nz + z) * CORES + c

    def t_peer(k):
        zz = lax.rem(z + k, nz)
        return zz, (x * nz + zz) * CORES + c

    def loop(lo, hi, f):
        def step(i, carry):
            f(i)
            return carry

        lax.fori_loop(lo, hi, step, 0)

    def push(src, dst, ssem, rsem, dev):
        pltpu.make_async_remote_copy(
            src_ref=src, dst_ref=dst, send_sem=ssem, recv_sem=rsem, device_id=dev, device_id_type=MESH
        ).start()

    def wait_recv(view, rsem):
        pltpu.make_async_remote_copy(
            src_ref=view, dst_ref=view, send_sem=send.at[0], recv_sem=rsem, device_id=(d, x), device_id_type=MESH
        ).wait_recv()

    def wait_send(view, ssem):
        pltpu.make_async_remote_copy(
            src_ref=view, dst_ref=view, send_sem=ssem, recv_sem=recv.at[0], device_id=(d, x), device_id_type=MESH
        ).wait_send()

    barrier = pltpu.get_barrier_semaphore()

    def greet(dev):
        pl.semaphore_signal(barrier, inc=1, device_id=dev, device_id_type=MESH)

    loop(1, nz, lambda k: greet((z_peer(k)[1], x)))
    loop(1, np_, lambda k: greet((p_peer(k)[1], x)))
    loop(1, nx, lambda k: greet((d, lax.rem(x + k, nx))))

    @pl.when(x != y)
    def _():
        loop(0, nz, lambda k: greet((t_peer(k)[1], y)))

    loads[0].wait()
    loads[1].wait()
    owner = owner_ref[...]
    owner_f = owner.astype(F32)
    sub, lane = iota((faces, faces), 0), iota((faces, faces), 1)
    owner_col = jnp.sum(jnp.where(sub == lane, owner_f, 0.0), axis=1, keepdims=True)
    rank = jnp.sum(
        jnp.where((owner_col == owner_f) & (sub < lane), 1.0, 0.0), axis=0, keepdims=True
    ).astype(jnp.int32)
    oc = owner & (CORES - 1)
    oz = (owner >> log2(CORES)) & (nz - 1)
    oy = owner >> log2(CORES * nz)
    place = ((oz * ny + oy) * CORES + oc) * cap + rank
    placed = iota((places, faces), 0) == place
    slot_col = (
        jnp.sum(jnp.where(placed, slot_ref[...].astype(F32) + 1.0, 0.0), axis=1, keepdims=True) - 1.0
    )
    spread = jnp.where(
        iota((places, lanes_m), 1) == (iota((places, lanes_m), 0) & (ma - 1)), slot_col, 0.0
    ).astype(BF16)
    by_z = one_hot(iota((nz, places), 0) == (iota((nz, places), 1) >> log2(ma)))
    meta = dot(by_z, spread)
    for i in range(nz):
        mout_a[i] = meta[i : i + 1, :]
    min_a[z] = mout_a[z]
    place_hot = one_hot(placed)

    def fill(i):
        part = dot(place_hot, face_ref[:, i * LANES : (i + 1) * LANES]).astype(BF16)
        out_a[i] = part.reshape(nz, ma, LANES)
        in_a[i, z] = out_a[i, z]

    loads[2].wait()
    fill(0)
    pl.semaphore_wait(barrier, (nz - 1) + (np_ - 1) + (nx - 1) + jnp.where(x == y, 0, nz))

    def send_meta(k):
        zz, dev = z_peer(k)
        push(mout_a.at[zz], min_a.at[z], send.at[0], recv.at[0], (dev, x))

    loop(1, nz, send_meta)

    def send_a(i):
        def step(k):
            zz, dev = z_peer(k)
            push(out_a.at[i, zz], in_a.at[i, z], send.at[1], recv_a.at[i], (dev, x))

        loop(1, nz, step)

    send_a(0)

    for i in range(1, ch):
        fill(i)
        send_a(i)
    for copy in loads[3:]:
        copy.wait()

    new, old = iota((ctx, ctx), 0), iota((ctx, ctx), 1)
    b_k, b_z, b_c = log2(kr), log2(nz), log2(CORES)
    o_k = old & (kr - 1)
    o_c = (old >> b_k) & (CORES - 1)
    o_z = (old >> (b_k + b_c)) & (nz - 1)
    o_y = old >> (b_k + b_c + b_z)
    perm_k = one_hot(new == ((o_c * ny + o_y) * nz + o_z) * kr + o_k)
    kp[...] = dot(perm_k, k_ref[...]).astype(BF16)
    vp[...] = dot(perm_k, v_ref[...]).astype(BF16)
    for h in range(heads):
        cols = slice(h * HD, (h + 1) * HD)
        scores = dot(q_ref[:, cols], kp[:, cols], NT) * scale
        top = jnp.max(scores, axis=-1, keepdims=True)
        e = jnp.exp(scores - top)
        w = e / jnp.sum(e, axis=-1, keepdims=True)
        wts[h] = w
        pb = w.astype(BF16)
        probs[h] = pb
        aall[x, :, cols] = dot(pb, vp[:, cols]).astype(BF16)

    def send_att(k):
        xx = lax.rem(x + k, nx)
        push(aall.at[x], aall.at[x], send.at[3], recv.at[2], (d, xx))

    loop(1, nx, send_att)

    new, old = iota((places, places), 0), iota((places, places), 1)
    o_r = old & (cap - 1)
    o_p = (old >> log2(cap)) & (np_ - 1)
    o_z = old >> log2(ma)
    perm_b[...] = one_hot(new == (o_p * nz + o_z) * cap + o_r)
    new, old = iota((dx, dx), 0), iota((dx, dx), 1)
    b_r = log2(rw)
    o_r = old & (rw - 1)
    o_c = (old >> b_r) & (CORES - 1)
    o_z = old >> (b_r + b_c)
    perm_w[...] = one_hot(new == (o_c * nz + o_z) * rw + o_r)

    wait_recv(min_a.at[pl.ds(0, nz - 1)], recv.at[0])
    for i in range(nz):
        m2d[i : i + 1, :] = min_a[i]
    min_b[p] = m2d[...]

    def send_mb(k):
        _, dev = p_peer(k)
        push(m2d, min_b.at[p], send.at[4], recv.at[3], (dev, x))

    loop(1, np_, send_mb)

    def forward(i):
        wait_recv(in_a.at[i, pl.ds(0, nz - 1)], recv_a.at[i])
        moved = dot(perm_b[...], in_a[i].reshape(places, LANES)).astype(BF16)
        out_b[i] = moved.reshape(np_, nz * cap, LANES)
        in_b[i, p] = out_b[i, p]

        def step(k):
            pp, dev = p_peer(k)
            push(out_b.at[i, pp], in_b.at[i, p], send.at[5], recv_b.at[i], (dev, x))

        loop(1, np_, step)

    forward(0)

    wait_recv(min_b.at[pl.ds(0, np_ - 1)], recv.at[3])
    pick = one_hot(
        iota((lanes_m, places), 0) == p * cap + (iota((lanes_m, places), 1) & (cap - 1))
    )
    table = dot(min_b[...].reshape(np_ * nz, lanes_m).astype(BF16), pick)
    slot_row = jnp.sum(
        jnp.where(
            iota((np_ * nz, places), 0) == (iota((np_ * nz, places), 1) >> log2(cap)), table, 0.0
        ),
        axis=0,
        keepdims=True,
    )
    land = one_hot(iota((tok, places), 0).astype(F32) == slot_row)
    gate = gate_ref[:, pl.ds(pl.multiple_of(x * dx, LANES), dx)]

    def landing(i):
        wait_recv(in_b.at[i, pl.ds(0, np_ - 1)], recv_b.at[i])
        grad_out = dot(land, in_b[i].reshape(places, LANES)).astype(BF16)
        bgx[i, x] = (gate[:, i * LANES : (i + 1) * LANES] * grad_out.astype(F32)).astype(BF16)

        def step(k):
            xx = lax.rem(x + k, nx)
            push(bgx.at[i, x], bgx.at[i, x], send.at[6], recv_x.at[i], (d, xx))

        loop(1, nx, step)

    def project(i):
        wait_recv(bgx.at[i, pl.ds(0, nx - 1)], recv_x.at[i])
        part = None
        for xx in range(nx):
            first = xx * dx + i * LANES
            term = dot(bgx[i, xx], w_ref[:, first : first + LANES], NT)
            part = term if part is None else part + term
        if i == 0:
            ga_acc[...] = part
        else:
            ga_acc[...] += part

    landing(0)

    wait_recv(aall.at[pl.ds(0, nx - 1)], recv.at[2])
    push(aall, asib, send.at[2], recv.at[1], (twin, x))

    for i in range(1, ch):
        forward(i)
        project(i - 1)
        landing(i)

    turned = None
    for i in range(ch):
        term = dot(perm_w[:, i * LANES : (i + 1) * LANES], bgx[i, x], NT)
        turned = term if turned is None else turned + term
    bgt[...] = turned.astype(BF16).reshape(CORES, nz * rw, tok)
    push(bgt.at[1 - c], bgt_in, send.at[7], recv.at[4], (twin, x))
    wait_recv(asib, recv.at[1])
    wait_recv(bgt_in, recv.at[4])

    def outer(xx):
        part = dot(bgt[c], aall[xx]) + dot(bgt_in[...], asib[xx])
        wo_out[xx] = part.astype(BF16).reshape(nz, rw, hw)

    loop(0, ny, outer)
    wo_in[y] = wo_out[y]

    def send_wo(k):
        yy, dev = y_peer(k)
        push(wo_out.at[yy], wo_in.at[y], send.at[8], recv.at[5], (dev, x))

    loop(1, ny, send_wo)

    project(ch - 1)
    ga = ga_acc[...].astype(BF16)
    for h in range(heads):
        cols = slice(h * HD, (h + 1) * HD)
        ga_h = ga[:, cols]
        gp = dot(ga_h, vp[:, cols], NT)
        w = wts[h]
        delta = jnp.sum(w * gp, axis=-1, keepdims=True)
        sg = (w * (gp - delta)).astype(BF16)
        gk_h = (scale * dot(sg, q_ref[:, cols], TN)).astype(BF16)
        gv_h = dot(probs[h], ga_h, TN).astype(BF16)
        kc_out[:, 0, :, :, cols] = gk_h.reshape(CORES, ny, nz * kr, HD)
        kc_out[:, 1, :, :, cols] = gv_h.reshape(CORES, ny, nz * kr, HD)
        gq_ref[:, cols] = (scale * dot(sg, kp[:, cols])).astype(BF16)
    push(kc_out.at[1 - c], kc_in, send.at[9], recv.at[6], (twin, x))

    wait_recv(kc_in, recv.at[6])

    def sum_kc(yy):
        for j in range(2):
            ky_out[yy, j] = (kc_out[c, j, yy].astype(F32) + kc_in[j, yy].astype(F32)).astype(BF16)

    loop(0, ny, sum_kc)
    ky_in[y] = ky_out[y]

    def send_ky(k):
        yy, dev = y_peer(k)
        push(ky_out.at[yy], ky_in.at[y], send.at[10], recv.at[9], (dev, x))

    loop(1, ny, send_ky)

    wait_recv(wo_in.at[pl.ds(0, ny - 1)], recv.at[5])

    def sum_wo(i):
        acc = wo_in[0, i].astype(F32)
        for j in range(1, ny):
            acc = acc + wo_in[j, i].astype(F32)
        wz_out[i] = acc.astype(BF16)

    loop(0, nz, sum_wo)

    def send_wz(k):
        zz, dev = t_peer(k)
        push(wz_out.at[zz], wz_in.at[z], send.at[11], recv.at[7], (dev, y))

    @pl.when(x != y)
    def _():
        send_wz(0)

    @pl.when(x == y)
    def _():
        wz_in[z] = wz_out[z]

    loop(1, nz, send_wz)

    wait_recv(ky_in.at[pl.ds(0, ny - 1)], recv.at[9])
    rows = 2 * halves * kr
    acc = None
    for j in range(2):
        tot = ky_in[0, j].astype(F32)
        for i in range(1, ny):
            tot = tot + ky_in[i, j].astype(F32)
        tot = tot.astype(BF16)
        for h in range(halves):
            r, s = iota((nz * rows, nz * kr), 0), iota((nz * rows, nz * kr), 1)
            inner = r & (rows - 1)
            sel = (
                ((r >> log2(rows)) == (s >> b_k))
                & ((inner >> b_k) == j * halves + h)
                & ((inner & (kr - 1)) == (s & (kr - 1)))
            )
            part = dot(one_hot(sel), tot[:, h * LANES : (h + 1) * LANES])
            acc = part if acc is None else acc + part
    kz_out[...] = acc.astype(BF16).reshape(nz, rows, LANES)
    kz_in[z] = kz_out[z]

    def send_kz(k):
        zz, dev = z_peer(k)
        push(kz_out.at[zz], kz_in.at[z], send.at[12], recv.at[8], (dev, x))

    loop(1, nz, send_kz)

    @pl.when(x != y)
    def _():
        wait_recv(wz_in, recv.at[7])

    @pl.when(x == y)
    def _():
        wait_recv(wz_in.at[pl.ds(0, nz - 1)], recv.at[7])

    acc = wz_in[0].astype(F32)
    for i in range(1, nz):
        acc = acc + wz_in[i].astype(F32)
    gwo_ref[...] = acc

    wait_recv(kz_in.at[pl.ds(0, nz - 1)], recv.at[8])
    acc = kz_in[0].astype(F32)
    for i in range(1, nz):
        acc = acc + kz_in[i].astype(F32)
    for h in range(halves):
        cols = slice(h * LANES, (h + 1) * LANES)
        gk_ref[:, cols] = acc[h * kr : (h + 1) * kr, :]
        gv_ref[:, cols] = acc[(halves + h) * kr : (halves + h + 1) * kr, :]

    wait_send(mout_a.at[pl.ds(0, nz - 1)], send.at[0])
    wait_send(out_a.at[:, pl.ds(0, nz - 1)], send.at[1])
    wait_send(aall, send.at[2])
    wait_send(aall.at[pl.ds(0, nx - 1)], send.at[3])
    wait_send(min_b.at[pl.ds(0, np_ - 1)], send.at[4])
    wait_send(out_b.at[:, pl.ds(0, np_ - 1)], send.at[5])
    wait_send(bgx.at[:, pl.ds(0, nx - 1)], send.at[6])
    wait_send(bgt_in, send.at[7])
    wait_send(wo_out.at[pl.ds(0, ny - 1)], send.at[8])
    wait_send(kc_in, send.at[9])
    wait_send(ky_out.at[pl.ds(0, ny - 1)], send.at[10])

    @pl.when(x != y)
    def _():
        wait_send(wz_out, send.at[11])

    @pl.when(x == y)
    def _():
        wait_send(wz_out.at[pl.ds(0, nz - 1)], send.at[11])

    wait_send(kz_out.at[pl.ds(0, nz - 1)], send.at[12])


def store(*refs):
    count = (len(refs) - 1) // 2
    done = refs[-1]
    copies = [
        pltpu.make_async_copy(refs[i], refs[count + i], done.at[i]) for i in range(count)
    ]
    for copy in copies:
        copy.start()
    for copy in copies:
        copy.wait()


def body(face_grads, face_owner, face_slot, queries, keys, values, w_out, branch_gate):
    nx = lax.axis_size("tensor")
    dp = lax.axis_size("dp")
    ny = nx
    nz = dp // (ny * CORES)
    np_ = ny * CORES
    faces, dx = face_grads.shape
    tok, hw = queries.shape
    ctx = keys.shape[0]
    heads = hw // HD
    cap = 2 * faces // dp
    ch = dx // LANES
    ma = np_ * cap
    places = nz * ma
    width = w_out.shape[1]
    rw = width // dp
    kr = ctx // dp
    rows = 2 * (hw // LANES) * kr
    lanes_m = max(LANES, ma)
    vmem = pltpu.VMEM
    dma = pltpu.SemaphoreType.DMA
    spec = pl.BlockSpec(memory_space=pltpu.VMEM)
    outs = (
        jax.ShapeDtypeStruct((tok, hw), BF16),
        jax.ShapeDtypeStruct((rw, hw), F32),
        jax.ShapeDtypeStruct((kr, hw), F32),
        jax.ShapeDtypeStruct((kr, hw), F32),
    )
    results = pl.pallas_call(
        functools.partial(kernel, nx, nz),
        out_shape=outs,
        in_specs=[pl.BlockSpec(memory_space=pltpu.HBM)] * 8,
        out_specs=(spec,) * 4,
        scratch_shapes=[
            vmem((ch, nz, ma, LANES), BF16),
            vmem((ch, nz, ma, LANES), BF16),
            vmem((nz, 1, lanes_m), F32),
            vmem((nz, 1, lanes_m), F32),
            vmem((nz, lanes_m), F32),
            vmem((np_, nz, lanes_m), F32),
            vmem((ch, np_, nz * cap, LANES), BF16),
            vmem((ch, np_, nz * cap, LANES), BF16),
            vmem((nx, tok, hw), BF16),
            vmem((nx, tok, hw), BF16),
            vmem((ch, nx, tok, LANES), BF16),
            vmem((CORES, nz * rw, tok), BF16),
            vmem((nz * rw, tok), BF16),
            vmem((ny, nz, rw, hw), BF16),
            vmem((ny, nz, rw, hw), BF16),
            vmem((nz, rw, hw), BF16),
            vmem((nz, rw, hw), BF16),
            vmem((CORES, 2, ny, nz * kr, hw), BF16),
            vmem((2, ny, nz * kr, hw), BF16),
            vmem((ny, 2, nz * kr, hw), BF16),
            vmem((ny, 2, nz * kr, hw), BF16),
            vmem((nz, rows, LANES), BF16),
            vmem((nz, rows, LANES), BF16),
            vmem((heads, tok, ctx), F32),
            vmem((heads, tok, ctx), BF16),
            vmem((ctx, hw), BF16),
            vmem((ctx, hw), BF16),
            vmem((tok, hw), F32),
            vmem((places, places), BF16),
            vmem((dx, dx), BF16),
            vmem((hw, width), BF16),
            vmem((faces, dx), BF16),
            vmem((1, faces), jnp.int32),
            vmem((1, faces), jnp.int32),
            vmem((tok, hw), BF16),
            vmem((ctx, hw), BF16),
            vmem((ctx, hw), BF16),
            vmem((1, width), F32),
            dma((8,)),
            dma((13,)),
            dma((ch,)),
            dma((ch,)),
            dma((ch,)),
            dma((10,)),
        ],
        compiler_params=pltpu.CompilerParams(
            collective_id=0, has_side_effects=True, vmem_limit_bytes=24 << 20
        ),
    )(
        *[
            pltpu.with_memory_space_constraint(a, pltpu.HBM)
            for a in (
                face_grads,
                face_owner.reshape(1, faces),
                face_slot.reshape(1, faces),
                queries,
                keys,
                values,
                w_out,
                branch_gate.reshape(1, width),
            )
        ]
    )
    return pl.pallas_call(
        store,
        out_shape=outs,
        in_specs=[spec] * 4,
        out_specs=(pl.BlockSpec(memory_space=pltpu.HBM),) * 4,
        scratch_shapes=[dma((4,))],
    )(*[pltpu.with_memory_space_constraint(r, pltpu.VMEM) for r in results])


def solution(mesh):
    in_specs = (
        P("dp", "tensor"),
        P("dp", None),
        P("dp", None),
        P("dp", "tensor"),
        P(None, "tensor"),
        P(None, "tensor"),
        P("tensor", None),
        P(),
    )
    out_specs = (P("dp", "tensor"), P("dp", "tensor"), P("dp", "tensor"), P("dp", "tensor"))
    return jax.shard_map(body, mesh=mesh, in_specs=in_specs, out_specs=out_specs, check_vma=False)
```

```python
import functools
import math

import jax
import jax.numpy as jnp
from jax import lax
from jax.experimental import pallas as pl
from jax.experimental.pallas import tpu as pltpu
from jax.sharding import PartitionSpec as P

HD = 128
LANES = 128
AHEAD = 3
CORES = 2
MESH = pl.DeviceIdType.MESH
F32 = jnp.float32
BF16 = jnp.bfloat16


def iota(shape, axis):
    return lax.broadcasted_iota(jnp.int32, shape, axis)


def log2(n):
    bits = n.bit_length() - 1
    assert 1 << bits == n
    return bits


def one_hot(cond):
    return jnp.where(cond, 1.0, 0.0).astype(BF16)


def dot(a, b, dims=((1,), (0,))):
    return lax.dot_general(a, b, (dims, ((), ())), preferred_element_type=F32)


NT = ((1,), (1,))
TN = ((0,), (0,))


def kernel(
    nx,
    nz,
    face_hbm,
    owner_hbm,
    slot_hbm,
    q_hbm,
    k_hbm,
    v_hbm,
    w_hbm,
    gate_hbm,
    gq_ref,
    gwo_ref,
    gk_ref,
    gv_ref,
    out_a,
    in_a,
    mout_a,
    min_a,
    m2d,
    min_b,
    out_b,
    in_b,
    aall,
    asib,
    bgx,
    bgt,
    bgt_in,
    wo_out,
    wo_in,
    wz_out,
    wz_in,
    wf_out,
    wf_in,
    kc_out,
    kc_in,
    ky_out,
    ky_in,
    kz_out,
    kz_in,
    wts,
    probs,
    kp,
    vp,
    ga_acc,
    perm_b,
    perm_w,
    w_ref,
    face_ref,
    owner_ref,
    slot_ref,
    q_ref,
    k_ref,
    v_ref,
    gate_ref,
    load,
    send,
    recv_a,
    recv_b,
    recv_x,
    recv_t,
    recv_w,
    recv_c,
    recv_y,
    recv,
):
    loads = [
        pltpu.make_async_copy(src, dst, load.at[i])
        for i, (src, dst) in enumerate(
            (
                (owner_hbm, owner_ref),
                (slot_hbm, slot_ref),
                (face_hbm, face_ref),
                (k_hbm, k_ref),
                (v_hbm, v_ref),
                (q_hbm, q_ref),
                (gate_hbm, gate_ref),
                (w_hbm, w_ref),
            )
        )
    ]
    ny = nx
    np_ = ny * CORES
    ch, _, ma, _ = out_a.shape
    faces, dx = face_ref.shape
    tok, hw = q_ref.shape
    ctx = k_ref.shape[0]
    heads = hw // HD
    places = nz * ma
    cap = ma // np_
    rw = gwo_ref.shape[0]
    kr = gk_ref.shape[0]
    halves = hw // LANES
    lanes_m = m2d.shape[1]
    scale = 1.0 / math.sqrt(HD)

    d = lax.axis_index("dp")
    x = lax.axis_index("tensor")
    c = lax.rem(d, CORES)
    z = lax.rem(lax.div(d, CORES), nz)
    y = lax.div(d, CORES * nz)
    p = y * CORES + c
    twin = d + 1 - 2 * c

    def z_peer(k):
        zz = lax.rem(z + k, nz)
        return zz, (y * nz + zz) * CORES + c

    def p_peer(k):
        pp = lax.rem(p + k, np_)
        return pp, (lax.div(pp, CORES) * nz + z) * CORES + lax.rem(pp, CORES)

    def y_peer(k):
        yy = lax.rem(y + k, ny)
        return yy, (yy * nz + z) * CORES + c

    mirror = ((x * nz + z) * CORES + c, y)

    def loop(lo, hi, f):
        def step(i, carry):
            f(i)
            return carry

        lax.fori_loop(lo, hi, step, 0)

    def far_first(f):
        half = nz // 2

        def step(j):
            f(jnp.where(lax.rem(j, 2) == 0, half + lax.div(j, 2), half - lax.div(j + 1, 2)))

        loop(0, nz - 1, step)

    def push(src, dst, ssem, rsem, dev):
        pltpu.make_async_remote_copy(
            src_ref=src, dst_ref=dst, send_sem=ssem, recv_sem=rsem, device_id=dev, device_id_type=MESH
        ).start()

    def wait_recv(view, rsem):
        pltpu.make_async_remote_copy(
            src_ref=view, dst_ref=view, send_sem=send.at[0], recv_sem=rsem, device_id=(d, x), device_id_type=MESH
        ).wait_recv()

    def wait_send(view, ssem):
        pltpu.make_async_remote_copy(
            src_ref=view, dst_ref=view, send_sem=ssem, recv_sem=recv.at[0], device_id=(d, x), device_id_type=MESH
        ).wait_send()

    barrier = pltpu.get_barrier_semaphore()

    def greet(dev):
        pl.semaphore_signal(barrier, inc=1, device_id=dev, device_id_type=MESH)

    far_first(lambda k: greet((z_peer(k)[1], x)))
    for copy in loads[:3]:
        copy.start()
    loop(1, np_, lambda k: greet((p_peer(k)[1], x)))
    loop(1, nx, lambda k: greet((d, lax.rem(x + k, nx))))

    @pl.when(x != y)
    def _():
        greet(mirror)

    for copy in loads[3:]:
        copy.start()

    loads[0].wait()
    loads[1].wait()
    owner = owner_ref[...]
    owner_f = owner.astype(F32)
    sub, lane = iota((faces, faces), 0), iota((faces, faces), 1)
    owner_col = jnp.sum(jnp.where(sub == lane, owner_f, 0.0), axis=1, keepdims=True)
    rank = jnp.sum(
        jnp.where((owner_col == owner_f) & (sub < lane), 1.0, 0.0), axis=0, keepdims=True
    ).astype(jnp.int32)
    oc = owner & (CORES - 1)
    oz = (owner >> log2(CORES)) & (nz - 1)
    oy = owner >> log2(CORES * nz)
    place = ((oz * ny + oy) * CORES + oc) * cap + rank
    placed = iota((places, faces), 0) == place
    slot_col = (
        jnp.sum(jnp.where(placed, slot_ref[...].astype(F32) + 1.0, 0.0), axis=1, keepdims=True) - 1.0
    )
    spread = jnp.where(
        iota((places, lanes_m), 1) == (iota((places, lanes_m), 0) & (ma - 1)), slot_col, 0.0
    ).astype(BF16)
    by_z = one_hot(iota((nz, places), 0) == (iota((nz, places), 1) >> log2(ma)))
    meta = dot(by_z, spread)
    for i in range(nz):
        mout_a[i] = meta[i : i + 1, :]
    min_a[z] = mout_a[z]
    place_hot = one_hot(placed)

    def fill(i):
        part = dot(place_hot, face_ref[:, i * LANES : (i + 1) * LANES]).astype(BF16)
        out_a[i] = part.reshape(nz, ma, LANES)
        in_a[i, z] = out_a[i, z]

    loads[2].wait()
    fill(0)
    pl.semaphore_wait(barrier, (nz - 1) + (np_ - 1) + (nx - 1) + jnp.where(x == y, 0, 1))

    def send_meta(k):
        zz, dev = z_peer(k)
        push(mout_a.at[zz], min_a.at[z], send.at[0], recv.at[0], (dev, x))

    far_first(send_meta)

    def send_a(i):
        def step(k):
            zz, dev = z_peer(k)
            push(out_a.at[i, zz], in_a.at[i, z], send.at[1], recv_a.at[i], (dev, x))

        far_first(step)

    send_a(0)

    for i in range(1, ch):
        fill(i)
        if i < AHEAD:
            send_a(i)
    for copy in loads[3:]:
        copy.wait()

    new, old = iota((ctx, ctx), 0), iota((ctx, ctx), 1)
    b_k, b_z, b_c = log2(kr), log2(nz), log2(CORES)
    o_k = old & (kr - 1)
    o_c = (old >> b_k) & (CORES - 1)
    o_z = (old >> (b_k + b_c)) & (nz - 1)
    o_y = old >> (b_k + b_c + b_z)
    perm_k = one_hot(new == ((o_c * ny + o_y) * nz + o_z) * kr + o_k)
    kp[...] = dot(perm_k, k_ref[...]).astype(BF16)
    vp[...] = dot(perm_k, v_ref[...]).astype(BF16)
    for h in range(heads):
        cols = slice(h * HD, (h + 1) * HD)
        scores = dot(kp[:, cols], q_ref[:, cols], NT) * scale
        top = jnp.max(scores, axis=0, keepdims=True)
        e = jnp.exp(scores - top)
        w = e / jnp.sum(e, axis=0, keepdims=True)
        wts[h] = w
        pb = w.astype(BF16)
        probs[h] = pb
        aall[x, :, cols] = dot(pb, vp[:, cols], TN).astype(BF16)

    def send_att(k):
        xx = lax.rem(x + k, nx)
        push(aall.at[x], aall.at[x], send.at[3], recv.at[2], (d, xx))

    loop(1, nx, send_att)

    new, old = iota((places, places), 0), iota((places, places), 1)
    o_r = old & (cap - 1)
    o_p = (old >> log2(cap)) & (np_ - 1)
    o_z = old >> log2(ma)
    perm_b[...] = one_hot(new == (o_p * nz + o_z) * cap + o_r)
    new, old = iota((LANES, LANES), 0), iota((LANES, LANES), 1)
    b_r = log2(rw)
    zc = LANES // (CORES * rw)
    o_r = old & (rw - 1)
    o_c = (old >> b_r) & (CORES - 1)
    o_z = old >> (b_r + b_c)
    perm_w[...] = one_hot(new == (o_c * zc + o_z) * rw + o_r)

    wait_recv(min_a.at[pl.ds(0, nz - 1)], recv.at[0])
    for i in range(nz):
        m2d[i : i + 1, :] = min_a[i]
    min_b[p] = m2d[...]

    def send_mb(k):
        _, dev = p_peer(k)
        push(m2d, min_b.at[p], send.at[4], recv.at[3], (dev, x))

    loop(1, np_, send_mb)

    def forward(i):
        wait_recv(in_a.at[i, pl.ds(0, nz - 1)], recv_a.at[i])
        if i + AHEAD < ch:
            send_a(i + AHEAD)
        moved = dot(perm_b[...], in_a[i].reshape(places, LANES)).astype(BF16)
        out_b[i] = moved.reshape(np_, nz * cap, LANES)
        in_b[i, p] = out_b[i, p]

        def step(k):
            pp, dev = p_peer(k)
            push(out_b.at[i, pp], in_b.at[i, p], send.at[5], recv_b.at[i], (dev, x))

        loop(1, np_, step)

    forward(0)

    wait_recv(min_b.at[pl.ds(0, np_ - 1)], recv.at[3])
    pick = one_hot(
        iota((lanes_m, places), 0) == p * cap + (iota((lanes_m, places), 1) & (cap - 1))
    )
    table = dot(min_b[...].reshape(np_ * nz, lanes_m).astype(BF16), pick)
    slot_row = jnp.sum(
        jnp.where(
            iota((np_ * nz, places), 0) == (iota((np_ * nz, places), 1) >> log2(cap)), table, 0.0
        ),
        axis=0,
        keepdims=True,
    )
    land = one_hot(iota((tok, places), 0).astype(F32) == slot_row)
    gate = gate_ref[:, pl.ds(pl.multiple_of(x * dx, LANES), dx)]

    def landing(i):
        wait_recv(in_b.at[i, pl.ds(0, np_ - 1)], recv_b.at[i])
        grad_out = dot(land, in_b[i].reshape(places, LANES)).astype(BF16)
        bgx[i, x] = (gate[:, i * LANES : (i + 1) * LANES] * grad_out.astype(F32)).astype(BF16)

        def step(k):
            xx = lax.rem(x + k, nx)
            push(bgx.at[i, x], bgx.at[i, x], send.at[6], recv_x.at[i], (d, xx))

        loop(1, nx, step)

    def project(i):
        wait_recv(bgx.at[i, pl.ds(0, nx - 1)], recv_x.at[i])
        part = None
        for xx in range(nx):
            first = xx * dx + i * LANES
            term = dot(bgx[i, xx], w_ref[:, first : first + LANES], NT)
            part = term if part is None else part + term
        if i == 0:
            ga_acc[...] = part
        else:
            ga_acc[...] += part

    def turn(i):
        bgt[i] = dot(perm_w[...], bgx[i, x], NT).astype(BF16).reshape(CORES, zc * rw, tok)
        push(bgt.at[i, 1 - c], bgt_in.at[i], send.at[7], recv_t.at[i], (twin, x))

    def outer(i):
        wait_recv(bgt_in.at[i], recv_t.at[i])
        for yy in range(ny):
            part = dot(bgt[i, c], aall[yy]) + dot(bgt_in[i], asib[yy])
            wo_out[i, yy] = part.astype(BF16).reshape(zc, rw, hw)
        wo_in[i, y] = wo_out[i, y]

        def step(k):
            yy, dev = y_peer(k)
            push(wo_out.at[i, yy], wo_in.at[i, y], send.at[8], recv_w.at[i], (dev, x))

        loop(1, ny, step)

    landing(0)
    turn(0)

    wait_recv(aall.at[pl.ds(0, nx - 1)], recv.at[2])
    push(aall, asib, send.at[2], recv.at[1], (twin, x))

    for i in range(1, ch):
        forward(i)
        if i == 1:
            wait_recv(asib, recv.at[1])
        outer(i - 1)
        project(i - 1)
        landing(i)
        turn(i)

    outer(ch - 1)
    project(ch - 1)
    ga = ga_acc[...].astype(BF16)
    score_grads = []
    for h in range(heads):
        cols = slice(h * HD, (h + 1) * HD)
        ga_h = ga[:, cols]
        gp = dot(vp[:, cols], ga_h, NT)
        w = wts[h]
        delta = jnp.sum(w * gp, axis=0, keepdims=True)
        sg = (w * (gp - delta)).astype(BF16)
        score_grads.append(sg)
        gk_h = (scale * dot(sg, q_ref[:, cols])).astype(BF16)
        gv_h = dot(probs[h], ga_h).astype(BF16)
        kc_out[h, :, 0] = gk_h.reshape(CORES, ny, nz * kr, HD)
        kc_out[h, :, 1] = gv_h.reshape(CORES, ny, nz * kr, HD)
        push(kc_out.at[h, 1 - c], kc_in.at[h], send.at[9], recv_c.at[h], (twin, x))

    def sum_wo(i):
        wait_recv(wo_in.at[i, pl.ds(0, ny - 1)], recv_w.at[i])

        def step(k):
            acc = wo_in[i, 0, k].astype(F32)
            for j in range(1, ny):
                acc = acc + wo_in[i, j, k].astype(F32)
            wz_out[i * zc + k] = acc.astype(BF16)

        loop(0, zc, step)

    for i in range(ch):
        sum_wo(i)
    wz_in[z] = wz_out[z]

    def send_wz(k):
        zz, dev = z_peer(k)
        push(wz_out.at[zz], wz_in.at[z], send.at[11], recv.at[7], (dev, x))

    far_first(send_wz)

    for h in range(heads):
        wait_recv(kc_in.at[h], recv_c.at[h])
        for yy in range(ny):
            for j in range(2):
                ky_out[h, yy, j] = (
                    kc_out[h, c, j, yy].astype(F32) + kc_in[h, j, yy].astype(F32)
                ).astype(BF16)
        ky_in[h, y] = ky_out[h, y]

        def send_ky(k, h=h):
            yy, dev = y_peer(k)
            push(ky_out.at[h, yy], ky_in.at[h, y], send.at[10], recv_y.at[h], (dev, x))

        loop(1, ny, send_ky)

    rows = 2 * halves * kr
    acc = None
    for h in range(heads):
        wait_recv(ky_in.at[h, pl.ds(0, ny - 1)], recv_y.at[h])
        for j in range(2):
            tot = ky_in[h, 0, j].astype(F32)
            for i in range(1, ny):
                tot = tot + ky_in[h, i, j].astype(F32)
            r, s = iota((nz * rows, nz * kr), 0), iota((nz * rows, nz * kr), 1)
            inner = r & (rows - 1)
            sel = (
                ((r >> log2(rows)) == (s >> b_k))
                & ((inner >> b_k) == j * halves + h)
                & ((inner & (kr - 1)) == (s & (kr - 1)))
            )
            part = dot(one_hot(sel), tot.astype(BF16))
            acc = part if acc is None else acc + part
    kz_out[...] = acc.astype(BF16).reshape(nz, rows, LANES)
    kz_in[z] = kz_out[z]

    def send_kz(k):
        zz, dev = z_peer(k)
        push(kz_out.at[zz], kz_in.at[z], send.at[12], recv.at[8], (dev, x))

    far_first(send_kz)

    wait_recv(wz_in.at[pl.ds(0, nz - 1)], recv.at[7])
    acc = wz_in[0].astype(F32)
    for i in range(1, nz):
        acc = acc + wz_in[i].astype(F32)
    wf_out[...] = acc

    @pl.when(x != y)
    def _():
        push(wf_out, wf_in, send.at[13], recv.at[6], mirror)

    @pl.when(x == y)
    def _():
        wf_in[...] = wf_out[...]

    for h in range(heads):
        cols = slice(h * HD, (h + 1) * HD)
        gq_ref[:, cols] = (scale * dot(score_grads[h], kp[:, cols], TN)).astype(BF16)

    wait_recv(kz_in.at[pl.ds(0, nz - 1)], recv.at[8])
    acc = kz_in[0].astype(F32)
    for i in range(1, nz):
        acc = acc + kz_in[i].astype(F32)
    for h in range(halves):
        cols = slice(h * LANES, (h + 1) * LANES)
        gk_ref[:, cols] = acc[h * kr : (h + 1) * kr, :]
        gv_ref[:, cols] = acc[(halves + h) * kr : (halves + h + 1) * kr, :]

    @pl.when(x != y)
    def _():
        wait_recv(wf_in, recv.at[6])

    gwo_ref[...] = wf_in[...]

    wait_send(mout_a.at[pl.ds(0, nz - 1)], send.at[0])
    wait_send(out_a.at[:, pl.ds(0, nz - 1)], send.at[1])
    wait_send(aall, send.at[2])
    wait_send(aall.at[pl.ds(0, nx - 1)], send.at[3])
    wait_send(min_b.at[pl.ds(0, np_ - 1)], send.at[4])
    wait_send(out_b.at[:, pl.ds(0, np_ - 1)], send.at[5])
    wait_send(bgx.at[:, pl.ds(0, nx - 1)], send.at[6])
    wait_send(bgt_in, send.at[7])
    wait_send(wo_out.at[:, pl.ds(0, ny - 1)], send.at[8])
    wait_send(kc_in, send.at[9])
    wait_send(ky_out.at[:, pl.ds(0, ny - 1)], send.at[10])

    wait_send(wz_out.at[pl.ds(0, nz - 1)], send.at[11])

    @pl.when(x != y)
    def _():
        wait_send(wf_out, send.at[13])

    wait_send(kz_out.at[pl.ds(0, nz - 1)], send.at[12])


def store(*refs):
    count = (len(refs) - 1) // 2
    done = refs[-1]
    copies = [
        pltpu.make_async_copy(refs[i], refs[count + i], done.at[i]) for i in range(count)
    ]
    for copy in copies:
        copy.start()
    for copy in copies:
        copy.wait()


def body(face_grads, face_owner, face_slot, queries, keys, values, w_out, branch_gate):
    nx = lax.axis_size("tensor")
    dp = lax.axis_size("dp")
    ny = nx
    nz = dp // (ny * CORES)
    np_ = ny * CORES
    faces, dx = face_grads.shape
    tok, hw = queries.shape
    ctx = keys.shape[0]
    heads = hw // HD
    cap = 2 * faces // dp
    ch = dx // LANES
    ma = np_ * cap
    places = nz * ma
    width = w_out.shape[1]
    rw = width // dp
    kr = ctx // dp
    rows = 2 * (hw // LANES) * kr
    lanes_m = max(LANES, ma)
    vmem = pltpu.VMEM
    dma = pltpu.SemaphoreType.DMA
    spec = pl.BlockSpec(memory_space=pltpu.VMEM)
    outs = (
        jax.ShapeDtypeStruct((tok, hw), BF16),
        jax.ShapeDtypeStruct((rw, hw), F32),
        jax.ShapeDtypeStruct((kr, hw), F32),
        jax.ShapeDtypeStruct((kr, hw), F32),
    )
    results = pl.pallas_call(
        functools.partial(kernel, nx, nz),
        out_shape=outs,
        in_specs=[pl.BlockSpec(memory_space=pltpu.HBM)] * 8,
        out_specs=(spec,) * 4,
        scratch_shapes=[
            vmem((ch, nz, ma, LANES), BF16),
            vmem((ch, nz, ma, LANES), BF16),
            vmem((nz, 1, lanes_m), F32),
            vmem((nz, 1, lanes_m), F32),
            vmem((nz, lanes_m), F32),
            vmem((np_, nz, lanes_m), F32),
            vmem((ch, np_, nz * cap, LANES), BF16),
            vmem((ch, np_, nz * cap, LANES), BF16),
            vmem((nx, tok, hw), BF16),
            vmem((nx, tok, hw), BF16),
            vmem((ch, nx, tok, LANES), BF16),
            vmem((ch, CORES, LANES // CORES, tok), BF16),
            vmem((ch, LANES // CORES, tok), BF16),
            vmem((ch, ny, nz // ch, rw, hw), BF16),
            vmem((ch, ny, nz // ch, rw, hw), BF16),
            vmem((nz, rw, hw), BF16),
            vmem((nz, rw, hw), BF16),
            vmem((rw, hw), F32),
            vmem((rw, hw), F32),
            vmem((heads, CORES, 2, ny, nz * kr, HD), BF16),
            vmem((heads, 2, ny, nz * kr, HD), BF16),
            vmem((heads, ny, 2, nz * kr, HD), BF16),
            vmem((heads, ny, 2, nz * kr, HD), BF16),
            vmem((nz, rows, LANES), BF16),
            vmem((nz, rows, LANES), BF16),
            vmem((heads, ctx, tok), F32),
            vmem((heads, ctx, tok), BF16),
            vmem((ctx, hw), BF16),
            vmem((ctx, hw), BF16),
            vmem((tok, hw), F32),
            vmem((places, places), BF16),
            vmem((LANES, LANES), BF16),
            vmem((hw, width), BF16),
            vmem((faces, dx), BF16),
            vmem((1, faces), jnp.int32),
            vmem((1, faces), jnp.int32),
            vmem((tok, hw), BF16),
            vmem((ctx, hw), BF16),
            vmem((ctx, hw), BF16),
            vmem((1, width), F32),
            dma((8,)),
            dma((14,)),
            dma((ch,)),
            dma((ch,)),
            dma((ch,)),
            dma((ch,)),
            dma((ch,)),
            dma((heads,)),
            dma((heads,)),
            dma((10,)),
        ],
        compiler_params=pltpu.CompilerParams(
            collective_id=0, has_side_effects=True, vmem_limit_bytes=24 << 20
        ),
    )(
        *[
            pltpu.with_memory_space_constraint(a, pltpu.HBM)
            for a in (
                face_grads,
                face_owner.reshape(1, faces),
                face_slot.reshape(1, faces),
                queries,
                keys,
                values,
                w_out,
                branch_gate.reshape(1, width),
            )
        ]
    )
    return pl.pallas_call(
        store,
        out_shape=outs,
        in_specs=[spec] * 4,
        out_specs=(pl.BlockSpec(memory_space=pltpu.HBM),) * 4,
        scratch_shapes=[dma((4,))],
    )(*[pltpu.with_memory_space_constraint(r, pltpu.VMEM) for r in results])


def solution(mesh):
    in_specs = (
        P("dp", "tensor"),
        P("dp", None),
        P("dp", None),
        P("dp", "tensor"),
        P(None, "tensor"),
        P(None, "tensor"),
        P("tensor", None),
        P(),
    )
    out_specs = (P("dp", "tensor"), P("dp", "tensor"), P("dp", "tensor"), P("dp", "tensor"))
    return jax.shard_map(body, mesh=mesh, in_specs=in_specs, out_specs=out_specs, check_vma=False)
```

```python
import functools
import math

import jax
import jax.numpy as jnp
from jax import lax
from jax.experimental import pallas as pl
from jax.experimental.pallas import tpu as pltpu
from jax.sharding import PartitionSpec as P

HD = 128
LANES = 128
AHEAD = 2
CORES = 2
MESH = pl.DeviceIdType.MESH
F32 = jnp.float32
BF16 = jnp.bfloat16


def iota(shape, axis):
    return lax.broadcasted_iota(jnp.int32, shape, axis)


def log2(n):
    bits = n.bit_length() - 1
    assert 1 << bits == n
    return bits


def one_hot(cond):
    return jnp.where(cond, 1.0, 0.0).astype(BF16)


def dot(a, b, dims=((1,), (0,))):
    return lax.dot_general(a, b, (dims, ((), ())), preferred_element_type=F32)


NT = ((1,), (1,))
TN = ((0,), (0,))


def kernel(
    nx,
    nz,
    face_hbm,
    owner_hbm,
    slot_hbm,
    q_hbm,
    k_hbm,
    v_hbm,
    w_hbm,
    gate_hbm,
    gq_ref,
    gwo_ref,
    gk_ref,
    gv_ref,
    out_a,
    in_a,
    mout_a,
    min_a,
    m2d,
    min_b,
    out_b,
    in_b,
    aall,
    asib,
    bgx,
    bgt,
    bgt_in,
    wo_out,
    wo_in,
    wz_out,
    wz_in,
    wf_out,
    wf_in,
    kc_out,
    kc_in,
    ky_out,
    ky_in,
    kz_out,
    kz_in,
    wts,
    probs,
    kp,
    vp,
    ga_acc,
    perm_b,
    perm_w,
    perm_k,
    w_ref,
    face_ref,
    owner_ref,
    slot_ref,
    q_ref,
    k_ref,
    v_ref,
    gate_ref,
    load,
    send,
    recv_a,
    recv_b,
    recv_x,
    recv_t,
    recv_w,
    recv_c,
    recv_y,
    recv,
):
    loads = [
        pltpu.make_async_copy(src, dst, load.at[i])
        for i, (src, dst) in enumerate(
            (
                (owner_hbm, owner_ref),
                (slot_hbm, slot_ref),
                (face_hbm, face_ref),
                (k_hbm, k_ref),
                (v_hbm, v_ref),
                (q_hbm, q_ref),
                (gate_hbm, gate_ref),
                (w_hbm, w_ref),
            )
        )
    ]
    ny = nx
    np_ = ny * CORES
    ch, _, ma, _ = out_a.shape
    faces, dx = face_ref.shape
    tok, hw = q_ref.shape
    ctx = k_ref.shape[0]
    heads = hw // HD
    places = nz * ma
    cap = ma // np_
    rw = gwo_ref.shape[0]
    kr = gk_ref.shape[0]
    halves = hw // LANES
    lanes_m = m2d.shape[1]
    scale = 1.0 / math.sqrt(HD)

    d = lax.axis_index("dp")
    x = lax.axis_index("tensor")
    c = lax.rem(d, CORES)
    z = lax.rem(lax.div(d, CORES), nz)
    y = lax.div(d, CORES * nz)
    p = y * CORES + c
    twin = d + 1 - 2 * c

    def z_peer(k):
        zz = lax.rem(z + k, nz)
        return zz, (y * nz + zz) * CORES + c

    def p_peer(k):
        pp = lax.rem(p + k, np_)
        return pp, (lax.div(pp, CORES) * nz + z) * CORES + lax.rem(pp, CORES)

    def y_peer(k):
        yy = lax.rem(y + k, ny)
        return yy, (yy * nz + z) * CORES + c

    mirror = ((x * nz + z) * CORES + c, y)

    def loop(lo, hi, f):
        def step(i, carry):
            f(i)
            return carry

        lax.fori_loop(lo, hi, step, 0)

    def far_first(f):
        half = nz // 2

        def step(j):
            f(jnp.where(lax.rem(j, 2) == 0, half + lax.div(j, 2), half - lax.div(j + 1, 2)))

        loop(0, nz - 1, step)

    def push(src, dst, ssem, rsem, dev):
        pltpu.make_async_remote_copy(
            src_ref=src, dst_ref=dst, send_sem=ssem, recv_sem=rsem, device_id=dev, device_id_type=MESH
        ).start()

    def wait_recv(view, rsem):
        pltpu.make_async_remote_copy(
            src_ref=view, dst_ref=view, send_sem=send.at[0], recv_sem=rsem, device_id=(d, x), device_id_type=MESH
        ).wait_recv()

    def wait_send(view, ssem):
        pltpu.make_async_remote_copy(
            src_ref=view, dst_ref=view, send_sem=ssem, recv_sem=recv.at[0], device_id=(d, x), device_id_type=MESH
        ).wait_send()

    barrier = pltpu.get_barrier_semaphore()

    def greet(dev):
        pl.semaphore_signal(barrier, inc=1, device_id=dev, device_id_type=MESH)

    far_first(lambda k: greet((z_peer(k)[1], x)))
    for copy in loads[:3]:
        copy.start()
    loop(1, np_, lambda k: greet((p_peer(k)[1], x)))
    loop(1, nx, lambda k: greet((d, lax.rem(x + k, nx))))

    @pl.when(x != y)
    def _():
        greet(mirror)

    for copy in loads[3:]:
        copy.start()

    loads[0].wait()
    loads[1].wait()
    owner = owner_ref[...]
    owner_f = owner.astype(F32)
    sub, lane = iota((faces, faces), 0), iota((faces, faces), 1)
    owner_col = jnp.sum(jnp.where(sub == lane, owner_f, 0.0), axis=1, keepdims=True)
    rank = jnp.sum(
        jnp.where((owner_col == owner_f) & (sub < lane), 1.0, 0.0), axis=0, keepdims=True
    ).astype(jnp.int32)
    oc = owner & (CORES - 1)
    oz = (owner >> log2(CORES)) & (nz - 1)
    oy = owner >> log2(CORES * nz)
    place = ((oz * ny + oy) * CORES + oc) * cap + rank
    placed = iota((places, faces), 0) == place
    slot_col = (
        jnp.sum(jnp.where(placed, slot_ref[...].astype(F32) + 1.0, 0.0), axis=1, keepdims=True) - 1.0
    )
    spread = jnp.where(
        iota((places, lanes_m), 1) == (iota((places, lanes_m), 0) & (ma - 1)), slot_col, 0.0
    ).astype(BF16)
    by_z = one_hot(iota((nz, places), 0) == (iota((nz, places), 1) >> log2(ma)))
    meta = dot(by_z, spread)
    for i in range(nz):
        mout_a[i] = meta[i : i + 1, :]
    min_a[z] = mout_a[z]
    place_hot = one_hot(placed)

    def fill(i):
        part = dot(place_hot, face_ref[:, i * LANES : (i + 1) * LANES]).astype(BF16)
        out_a[i] = part.reshape(nz, ma, LANES)
        in_a[i, z] = out_a[i, z]

    loads[2].wait()
    fill(0)
    pl.semaphore_wait(barrier, (nz - 1) + (np_ - 1) + (nx - 1) + jnp.where(x == y, 0, 1))

    def send_meta(k):
        zz, dev = z_peer(k)
        push(mout_a.at[zz], min_a.at[z], send.at[0], recv.at[0], (dev, x))

    far_first(send_meta)

    def send_a(i):
        def step(k):
            zz, dev = z_peer(k)
            push(out_a.at[i, zz], in_a.at[i, z], send.at[1], recv_a.at[i], (dev, x))

        far_first(step)

    send_a(0)

    for i in range(1, ch):
        fill(i)
        if i < AHEAD:
            send_a(i)
    for copy in loads[3:]:
        copy.wait()

    new, old = iota((ctx, ctx), 0), iota((ctx, ctx), 1)
    b_k, b_z, b_c = log2(kr), log2(nz), log2(CORES)
    o_k = old & (kr - 1)
    o_c = (old >> b_k) & (CORES - 1)
    o_z = (old >> (b_k + b_c)) & (nz - 1)
    o_y = old >> (b_k + b_c + b_z)
    reorder = one_hot(new == ((o_c * ny + o_y) * nz + o_z) * kr + o_k)
    kp[...] = dot(reorder, k_ref[...]).astype(BF16)
    vp[...] = dot(reorder, v_ref[...]).astype(BF16)
    for h in range(heads):
        cols = slice(h * HD, (h + 1) * HD)
        scores = dot(kp[:, cols], q_ref[:, cols], NT) * scale
        top = jnp.max(scores, axis=0, keepdims=True)
        e = jnp.exp(scores - top)
        w = e / jnp.sum(e, axis=0, keepdims=True)
        wts[h] = w
        pb = w.astype(BF16)
        probs[h] = pb
        aall[x, :, cols] = dot(pb, vp[:, cols], TN).astype(BF16)

    def send_att(k):
        xx = lax.rem(x + k, nx)
        push(aall.at[x], aall.at[x], send.at[3], recv.at[2], (d, xx))

    loop(1, nx, send_att)

    new, old = iota((places, places), 0), iota((places, places), 1)
    o_r = old & (cap - 1)
    o_p = (old >> log2(cap)) & (np_ - 1)
    o_z = old >> log2(ma)
    perm_b[...] = one_hot(new == (o_p * nz + o_z) * cap + o_r)
    rows = 2 * halves * kr
    new, old = iota((nz * rows, nz * kr), 0), iota((nz * rows, nz * kr), 1)
    inner = new & (rows - 1)
    for i in range(2 * halves):
        perm_k[i] = one_hot(
            ((new >> log2(rows)) == (old >> b_k))
            & ((inner >> b_k) == i)
            & ((inner & (kr - 1)) == (old & (kr - 1)))
        )
    new, old = iota((LANES, LANES), 0), iota((LANES, LANES), 1)
    b_r = log2(rw)
    zc = LANES // (CORES * rw)
    o_r = old & (rw - 1)
    o_c = (old >> b_r) & (CORES - 1)
    o_z = old >> (b_r + b_c)
    perm_w[...] = one_hot(new == (o_c * zc + o_z) * rw + o_r)

    wait_recv(min_a.at[pl.ds(0, nz - 1)], recv.at[0])
    for i in range(nz):
        m2d[i : i + 1, :] = min_a[i]
    min_b[p] = m2d[...]

    def send_mb(k):
        _, dev = p_peer(k)
        push(m2d, min_b.at[p], send.at[4], recv.at[3], (dev, x))

    loop(1, np_, send_mb)

    def forward(i):
        wait_recv(in_a.at[i, pl.ds(0, nz - 1)], recv_a.at[i])
        if i + AHEAD < ch:
            send_a(i + AHEAD)
        moved = dot(perm_b[...], in_a[i].reshape(places, LANES)).astype(BF16)
        out_b[i] = moved.reshape(np_, nz * cap, LANES)
        in_b[i, p] = out_b[i, p]

        for k in sorted(range(1, np_), key=lambda k: abs(k - np_ // 2)):
            pp, dev = p_peer(k)
            push(out_b.at[i, pp], in_b.at[i, p], send.at[5], recv_b.at[i], (dev, x))

    forward(0)

    wait_recv(min_b.at[pl.ds(0, np_ - 1)], recv.at[3])
    pick = one_hot(
        iota((lanes_m, places), 0) == p * cap + (iota((lanes_m, places), 1) & (cap - 1))
    )
    table = dot(min_b[...].reshape(np_ * nz, lanes_m).astype(BF16), pick)
    slot_row = jnp.sum(
        jnp.where(
            iota((np_ * nz, places), 0) == (iota((np_ * nz, places), 1) >> log2(cap)), table, 0.0
        ),
        axis=0,
        keepdims=True,
    )
    land = one_hot(iota((tok, places), 0).astype(F32) == slot_row)
    gate = gate_ref[:, pl.ds(pl.multiple_of(x * dx, LANES), dx)]

    def landing(i):
        wait_recv(in_b.at[i, pl.ds(0, np_ - 1)], recv_b.at[i])
        grad_out = dot(land, in_b[i].reshape(places, LANES)).astype(BF16)
        bgx[i, x] = (gate[:, i * LANES : (i + 1) * LANES] * grad_out.astype(F32)).astype(BF16)

        for k in sorted(range(1, nx), key=lambda k: abs(k - nx // 2)):
            xx = lax.rem(x + k, nx)
            push(bgx.at[i, x], bgx.at[i, x], send.at[6], recv_x.at[i], (d, xx))

    def project(i):
        wait_recv(bgx.at[i, pl.ds(0, nx - 1)], recv_x.at[i])
        part = ga_acc[...] if i else None
        for xx in range(nx):
            first = xx * dx + i * LANES
            term = dot(bgx[i, xx], w_ref[:, first : first + LANES], NT)
            part = term if part is None else part + term
        ga_acc[...] = part

    def turn(i):
        bgt[i] = dot(perm_w[...], bgx[i, x], NT).astype(BF16).reshape(CORES, zc * rw, tok)
        push(bgt.at[i, 1 - c], bgt_in.at[i], send.at[7], recv_t.at[i], (twin, x))

    def outer(i):
        wait_recv(bgt_in.at[i], recv_t.at[i])
        for yy in range(ny):
            part = dot(bgt[i, c], aall[yy]) + dot(bgt_in[i], asib[yy])
            wo_out[i, yy] = part.astype(BF16).reshape(zc, rw, hw)
        wo_in[i, y] = wo_out[i, y]

        def step(k):
            yy, dev = y_peer(k)
            push(wo_out.at[i, yy], wo_in.at[i, y], send.at[8], recv_w.at[i], (dev, x))

        loop(1, ny, step)

    landing(0)
    turn(0)

    wait_recv(aall.at[pl.ds(0, nx - 1)], recv.at[2])
    push(aall, asib, send.at[2], recv.at[1], (twin, x))

    for i in range(1, ch):
        forward(i)
        if i == 1:
            wait_recv(asib, recv.at[1])
        outer(i - 1)
        project(i - 1)
        landing(i)
        turn(i)

    outer(ch - 1)
    project(ch - 1)
    ga = ga_acc[...].astype(BF16)
    score_grads = []
    for h in range(heads):
        cols = slice(h * HD, (h + 1) * HD)
        ga_h = ga[:, cols]
        gp = dot(vp[:, cols], ga_h, NT)
        w = wts[h]
        delta = jnp.sum(w * gp, axis=0, keepdims=True)
        sg = (w * (gp - delta)).astype(BF16)
        score_grads.append(sg)
        gk_h = (scale * dot(sg, q_ref[:, cols])).astype(BF16)
        gv_h = dot(probs[h], ga_h).astype(BF16)
        kc_out[h, :, 0] = gk_h.reshape(CORES, ny, nz * kr, HD)
        kc_out[h, :, 1] = gv_h.reshape(CORES, ny, nz * kr, HD)
        push(kc_out.at[h, 1 - c], kc_in.at[h], send.at[9], recv_c.at[h], (twin, x))

    def sum_wo(i):
        wait_recv(wo_in.at[i, pl.ds(0, ny - 1)], recv_w.at[i])

        def step(k):
            acc = wo_in[i, 0, k].astype(F32)
            for j in range(1, ny):
                acc = acc + wo_in[i, j, k].astype(F32)
            wz_out[i * zc + k] = acc.astype(BF16)

        loop(0, zc, step)

    for i in range(ch):
        sum_wo(i)
    wz_in[z] = wz_out[z]

    def send_wz(k):
        zz, dev = z_peer(k)
        push(wz_out.at[zz], wz_in.at[z], send.at[11], recv.at[7], (dev, x))

    far_first(send_wz)

    for h in range(heads):
        wait_recv(kc_in.at[h], recv_c.at[h])
        for yy in range(ny):
            for j in range(2):
                ky_out[h, yy, j] = (
                    kc_out[h, c, j, yy].astype(F32) + kc_in[h, j, yy].astype(F32)
                ).astype(BF16)
        ky_in[h, y] = ky_out[h, y]

        for k in sorted(range(1, ny), key=lambda k: abs(k - ny // 2)):
            yy, dev = y_peer(k)
            push(ky_out.at[h, yy], ky_in.at[h, y], send.at[10], recv_y.at[h], (dev, x))

    acc = None
    for h in range(heads):
        wait_recv(ky_in.at[h, pl.ds(0, ny - 1)], recv_y.at[h])
        for j in range(2):
            tot = ky_in[h, 0, j].astype(F32)
            for i in range(1, ny):
                tot = tot + ky_in[h, i, j].astype(F32)
            part = dot(perm_k[j * halves + h], tot.astype(BF16))
            acc = part if acc is None else acc + part
    kz_out[...] = acc.astype(BF16).reshape(nz, rows, LANES)
    kz_in[z] = kz_out[z]

    def send_kz(k):
        zz, dev = z_peer(k)
        push(kz_out.at[zz], kz_in.at[z], send.at[12], recv.at[8], (dev, x))

    far_first(send_kz)

    wait_recv(wz_in.at[pl.ds(0, nz - 1)], recv.at[7])
    acc = wz_in[0].astype(F32)
    for i in range(1, nz):
        acc = acc + wz_in[i].astype(F32)
    wf_out[...] = acc

    @pl.when(x != y)
    def _():
        push(wf_out, wf_in, send.at[13], recv.at[6], mirror)

    @pl.when(x == y)
    def _():
        wf_in[...] = wf_out[...]

    for h in range(heads):
        cols = slice(h * HD, (h + 1) * HD)
        gq_ref[:, cols] = (scale * dot(score_grads[h], kp[:, cols], TN)).astype(BF16)

    wait_recv(kz_in.at[pl.ds(0, nz - 1)], recv.at[8])
    acc = kz_in[0].astype(F32)
    for i in range(1, nz):
        acc = acc + kz_in[i].astype(F32)
    for h in range(halves):
        cols = slice(h * LANES, (h + 1) * LANES)
        gk_ref[:, cols] = acc[h * kr : (h + 1) * kr, :]
        gv_ref[:, cols] = acc[(halves + h) * kr : (halves + h + 1) * kr, :]

    @pl.when(x != y)
    def _():
        wait_recv(wf_in, recv.at[6])

    gwo_ref[...] = wf_in[...]

    wait_send(mout_a.at[pl.ds(0, nz - 1)], send.at[0])
    wait_send(out_a.at[:, pl.ds(0, nz - 1)], send.at[1])
    wait_send(aall, send.at[2])
    wait_send(aall.at[pl.ds(0, nx - 1)], send.at[3])
    wait_send(min_b.at[pl.ds(0, np_ - 1)], send.at[4])
    wait_send(out_b.at[:, pl.ds(0, np_ - 1)], send.at[5])
    wait_send(bgx.at[:, pl.ds(0, nx - 1)], send.at[6])
    wait_send(bgt_in, send.at[7])
    wait_send(wo_out.at[:, pl.ds(0, ny - 1)], send.at[8])
    wait_send(kc_in, send.at[9])
    wait_send(ky_out.at[:, pl.ds(0, ny - 1)], send.at[10])

    wait_send(wz_out.at[pl.ds(0, nz - 1)], send.at[11])

    @pl.when(x != y)
    def _():
        wait_send(wf_out, send.at[13])

    wait_send(kz_out.at[pl.ds(0, nz - 1)], send.at[12])


def store(*refs):
    count = (len(refs) - 1) // 2
    done = refs[-1]
    copies = [
        pltpu.make_async_copy(refs[i], refs[count + i], done.at[i]) for i in range(count)
    ]
    for copy in copies:
        copy.start()
    for copy in copies:
        copy.wait()


def body(face_grads, face_owner, face_slot, queries, keys, values, w_out, branch_gate):
    nx = lax.axis_size("tensor")
    dp = lax.axis_size("dp")
    ny = nx
    nz = dp // (ny * CORES)
    np_ = ny * CORES
    faces, dx = face_grads.shape
    tok, hw = queries.shape
    ctx = keys.shape[0]
    heads = hw // HD
    cap = 2 * faces // dp
    ch = dx // LANES
    ma = np_ * cap
    places = nz * ma
    width = w_out.shape[1]
    rw = width // dp
    kr = ctx // dp
    rows = 2 * (hw // LANES) * kr
    lanes_m = max(LANES, ma)
    vmem = pltpu.VMEM
    dma = pltpu.SemaphoreType.DMA
    spec = pl.BlockSpec(memory_space=pltpu.VMEM)
    outs = (
        jax.ShapeDtypeStruct((tok, hw), BF16),
        jax.ShapeDtypeStruct((rw, hw), F32),
        jax.ShapeDtypeStruct((kr, hw), F32),
        jax.ShapeDtypeStruct((kr, hw), F32),
    )
    results = pl.pallas_call(
        functools.partial(kernel, nx, nz),
        out_shape=outs,
        in_specs=[pl.BlockSpec(memory_space=pltpu.HBM)] * 8,
        out_specs=(spec,) * 4,
        scratch_shapes=[
            vmem((ch, nz, ma, LANES), BF16),
            vmem((ch, nz, ma, LANES), BF16),
            vmem((nz, 1, lanes_m), F32),
            vmem((nz, 1, lanes_m), F32),
            vmem((nz, lanes_m), F32),
            vmem((np_, nz, lanes_m), F32),
            vmem((ch, np_, nz * cap, LANES), BF16),
            vmem((ch, np_, nz * cap, LANES), BF16),
            vmem((nx, tok, hw), BF16),
            vmem((nx, tok, hw), BF16),
            vmem((ch, nx, tok, LANES), BF16),
            vmem((ch, CORES, LANES // CORES, tok), BF16),
            vmem((ch, LANES // CORES, tok), BF16),
            vmem((ch, ny, nz // ch, rw, hw), BF16),
            vmem((ch, ny, nz // ch, rw, hw), BF16),
            vmem((nz, rw, hw), BF16),
            vmem((nz, rw, hw), BF16),
            vmem((rw, hw), F32),
            vmem((rw, hw), F32),
            vmem((heads, CORES, 2, ny, nz * kr, HD), BF16),
            vmem((heads, 2, ny, nz * kr, HD), BF16),
            vmem((heads, ny, 2, nz * kr, HD), BF16),
            vmem((heads, ny, 2, nz * kr, HD), BF16),
            vmem((nz, rows, LANES), BF16),
            vmem((nz, rows, LANES), BF16),
            vmem((heads, ctx, tok), F32),
            vmem((heads, ctx, tok), BF16),
            vmem((ctx, hw), BF16),
            vmem((ctx, hw), BF16),
            vmem((tok, hw), F32),
            vmem((places, places), BF16),
            vmem((LANES, LANES), BF16),
            vmem((2 * (hw // LANES), nz * rows, nz * kr), BF16),
            vmem((hw, width), BF16),
            vmem((faces, dx), BF16),
            vmem((1, faces), jnp.int32),
            vmem((1, faces), jnp.int32),
            vmem((tok, hw), BF16),
            vmem((ctx, hw), BF16),
            vmem((ctx, hw), BF16),
            vmem((1, width), F32),
            dma((8,)),
            dma((14,)),
            dma((ch,)),
            dma((ch,)),
            dma((ch,)),
            dma((ch,)),
            dma((ch,)),
            dma((heads,)),
            dma((heads,)),
            dma((10,)),
        ],
        compiler_params=pltpu.CompilerParams(
            collective_id=0, has_side_effects=True, vmem_limit_bytes=24 << 20
        ),
    )(
        *[
            pltpu.with_memory_space_constraint(a, pltpu.HBM)
            for a in (
                face_grads,
                face_owner.reshape(1, faces),
                face_slot.reshape(1, faces),
                queries,
                keys,
                values,
                w_out,
                branch_gate.reshape(1, width),
            )
        ]
    )
    return pl.pallas_call(
        store,
        out_shape=outs,
        in_specs=[spec] * 4,
        out_specs=(pl.BlockSpec(memory_space=pltpu.HBM),) * 4,
        scratch_shapes=[dma((4,))],
    )(*[pltpu.with_memory_space_constraint(r, pltpu.VMEM) for r in results])


def solution(mesh):
    in_specs = (
        P("dp", "tensor"),
        P("dp", None),
        P("dp", None),
        P("dp", "tensor"),
        P(None, "tensor"),
        P(None, "tensor"),
        P("tensor", None),
        P(),
    )
    out_specs = (P("dp", "tensor"), P("dp", "tensor"), P("dp", "tensor"), P("dp", "tensor"))
    return jax.shard_map(body, mesh=mesh, in_specs=in_specs, out_specs=out_specs, check_vma=False)
```

```python
import functools
import math

import jax
import jax.numpy as jnp
from jax import lax
from jax.experimental import pallas as pl
from jax.experimental.pallas import tpu as pltpu
from jax.sharding import PartitionSpec as P

HD = 128
LANES = 128
AHEAD = 2
CORES = 2
MESH = pl.DeviceIdType.MESH
F32 = jnp.float32
BF16 = jnp.bfloat16


def iota(shape, axis):
    return lax.broadcasted_iota(jnp.int32, shape, axis)


def log2(n):
    bits = n.bit_length() - 1
    assert 1 << bits == n
    return bits


def one_hot(cond):
    return jnp.where(cond, 1.0, 0.0).astype(BF16)


def dot(a, b, dims=((1,), (0,))):
    return lax.dot_general(a, b, (dims, ((), ())), preferred_element_type=F32)


NT = ((1,), (1,))
TN = ((0,), (0,))


def kernel(
    nx,
    nz,
    face_hbm,
    owner_hbm,
    slot_hbm,
    q_hbm,
    k_hbm,
    v_hbm,
    w_hbm,
    gate_hbm,
    gq_ref,
    gwo_ref,
    gk_ref,
    gv_ref,
    out_a,
    in_a,
    mout_a,
    min_a,
    m2d,
    min_b,
    out_b,
    in_b,
    aall,
    asib,
    bgx,
    bgt,
    bgt_in,
    wo_out,
    wo_in,
    wz_out,
    wz_in,
    wf_out,
    wf_in,
    kc_out,
    kc_in,
    ky_out,
    ky_in,
    kz_out,
    kz_in,
    wts,
    probs,
    kp,
    vp,
    ga_acc,
    perm_b,
    perm_w,
    perm_k,
    w_ref,
    face_ref,
    owner_ref,
    slot_ref,
    q_ref,
    k_ref,
    v_ref,
    gate_ref,
    load,
    send,
    recv_a,
    recv_b,
    recv_x,
    recv_t,
    recv_w,
    recv_c,
    recv_y,
    recv,
):
    loads = [
        pltpu.make_async_copy(src, dst, load.at[i])
        for i, (src, dst) in enumerate(
            (
                (owner_hbm, owner_ref),
                (slot_hbm, slot_ref),
                (face_hbm, face_ref),
                (k_hbm, k_ref),
                (v_hbm, v_ref),
                (q_hbm, q_ref),
                (gate_hbm, gate_ref),
                (w_hbm, w_ref),
            )
        )
    ]
    ny = nx
    np_ = ny * CORES
    ch, _, ma, _ = out_a.shape
    faces, dx = face_ref.shape
    tok, hw = q_ref.shape
    ctx = k_ref.shape[0]
    heads = hw // HD
    places = nz * ma
    cap = ma // np_
    rw = gwo_ref.shape[0]
    kr = gk_ref.shape[0]
    halves = hw // LANES
    lanes_m = m2d.shape[1]
    scale = 1.0 / math.sqrt(HD)

    d = lax.axis_index("dp")
    x = lax.axis_index("tensor")
    c = lax.rem(d, CORES)
    z = lax.rem(lax.div(d, CORES), nz)
    y = lax.div(d, CORES * nz)
    p = y * CORES + c
    twin = d + 1 - 2 * c

    def z_peer(k):
        zz = lax.rem(z + k, nz)
        return zz, (y * nz + zz) * CORES + c

    def p_peer(k):
        pp = lax.rem(p + k, np_)
        return pp, (lax.div(pp, CORES) * nz + z) * CORES + lax.rem(pp, CORES)

    def y_peer(k):
        yy = lax.rem(y + k, ny)
        return yy, (yy * nz + z) * CORES + c

    mirror = ((x * nz + z) * CORES + c, y)

    def loop(lo, hi, f):
        def step(i, carry):
            f(i)
            return carry

        lax.fori_loop(lo, hi, step, 0)

    def far_first(f):
        half = nz // 2

        def step(j):
            f(jnp.where(lax.rem(j, 2) == 0, half + lax.div(j, 2), half - lax.div(j + 1, 2)))

        loop(0, nz - 1, step)

    def push(src, dst, ssem, rsem, dev):
        pltpu.make_async_remote_copy(
            src_ref=src, dst_ref=dst, send_sem=ssem, recv_sem=rsem, device_id=dev, device_id_type=MESH
        ).start()

    def wait_recv(view, rsem):
        pltpu.make_async_remote_copy(
            src_ref=view, dst_ref=view, send_sem=send.at[0], recv_sem=rsem, device_id=(d, x), device_id_type=MESH
        ).wait_recv()

    def wait_send(view, ssem):
        pltpu.make_async_remote_copy(
            src_ref=view, dst_ref=view, send_sem=ssem, recv_sem=recv.at[0], device_id=(d, x), device_id_type=MESH
        ).wait_send()

    barrier = pltpu.get_barrier_semaphore()

    def greet(dev):
        pl.semaphore_signal(barrier, inc=1, device_id=dev, device_id_type=MESH)

    far_first(lambda k: greet((z_peer(k)[1], x)))
    for copy in loads[:3]:
        copy.start()
    loop(1, np_, lambda k: greet((p_peer(k)[1], x)))
    loop(1, nx, lambda k: greet((d, lax.rem(x + k, nx))))

    @pl.when(x != y)
    def _():
        greet(mirror)

    for copy in loads[3:]:
        copy.start()

    loads[0].wait()
    loads[1].wait()
    owner = owner_ref[...]
    owner_f = owner.astype(F32)
    sub, lane = iota((faces, faces), 0), iota((faces, faces), 1)
    owner_col = jnp.sum(jnp.where(sub == lane, owner_f, 0.0), axis=1, keepdims=True)
    rank = jnp.sum(
        jnp.where((owner_col == owner_f) & (sub < lane), 1.0, 0.0), axis=0, keepdims=True
    ).astype(jnp.int32)
    oc = owner & (CORES - 1)
    oz = (owner >> log2(CORES)) & (nz - 1)
    oy = owner >> log2(CORES * nz)
    place = ((oz * ny + oy) * CORES + oc) * cap + rank
    placed = iota((places, faces), 0) == place
    slot_col = (
        jnp.sum(jnp.where(placed, slot_ref[...].astype(F32) + 1.0, 0.0), axis=1, keepdims=True) - 1.0
    )
    spread = jnp.where(
        iota((places, lanes_m), 1) == (iota((places, lanes_m), 0) & (ma - 1)), slot_col, 0.0
    ).astype(BF16)
    by_z = one_hot(iota((nz, places), 0) == (iota((nz, places), 1) >> log2(ma)))
    meta = dot(by_z, spread)
    for i in range(nz):
        mout_a[i] = meta[i : i + 1, :]
    min_a[z] = mout_a[z]
    place_hot = one_hot(placed)

    def fill(i):
        part = dot(place_hot, face_ref[:, i * LANES : (i + 1) * LANES]).astype(BF16)
        out_a[i] = part.reshape(nz, ma, LANES)
        in_a[i, z] = out_a[i, z]

    loads[2].wait()
    fill(0)
    pl.semaphore_wait(barrier, (nz - 1) + (np_ - 1) + (nx - 1) + jnp.where(x == y, 0, 1))

    def send_meta(k):
        zz, dev = z_peer(k)
        push(mout_a.at[zz], min_a.at[z], send.at[0], recv.at[0], (dev, x))

    far_first(send_meta)

    def send_a(i):
        def step(k):
            zz, dev = z_peer(k)
            push(out_a.at[i, zz], in_a.at[i, z], send.at[1], recv_a.at[i], (dev, x))

        far_first(step)

    send_a(0)

    for i in range(1, ch):
        fill(i)
        if i < AHEAD:
            send_a(i)
    for copy in loads[3:]:
        copy.wait()

    new, old = iota((ctx, ctx), 0), iota((ctx, ctx), 1)
    b_k, b_z, b_c = log2(kr), log2(nz), log2(CORES)
    o_k = old & (kr - 1)
    o_c = (old >> b_k) & (CORES - 1)
    o_z = (old >> (b_k + b_c)) & (nz - 1)
    o_y = old >> (b_k + b_c + b_z)
    reorder = one_hot(new == ((o_c * ny + o_y) * nz + o_z) * kr + o_k)
    kp[...] = dot(reorder, k_ref[...]).astype(BF16)
    vp[...] = dot(reorder, v_ref[...]).astype(BF16)
    for h in range(heads):
        cols = slice(h * HD, (h + 1) * HD)
        scores = dot(kp[:, cols], q_ref[:, cols], NT) * scale
        top = jnp.max(scores, axis=0, keepdims=True)
        e = jnp.exp(scores - top)
        w = e / jnp.sum(e, axis=0, keepdims=True)
        wts[h] = w
        pb = w.astype(BF16)
        probs[h] = pb
        aall[x, :, cols] = dot(pb, vp[:, cols], TN).astype(BF16)

    def send_att(k):
        xx = lax.rem(x + k, nx)
        push(aall.at[x], aall.at[x], send.at[3], recv.at[2], (d, xx))

    loop(1, nx, send_att)

    new, old = iota((places, places), 0), iota((places, places), 1)
    o_r = old & (cap - 1)
    o_p = (old >> log2(cap)) & (np_ - 1)
    o_z = old >> log2(ma)
    perm_b[...] = one_hot(new == (o_p * nz + o_z) * cap + o_r)
    rows = 2 * halves * kr
    new, old = iota((nz * rows, nz * kr), 0), iota((nz * rows, nz * kr), 1)
    inner = new & (rows - 1)
    for i in range(2 * halves):
        perm_k[i] = one_hot(
            ((new >> log2(rows)) == (old >> b_k))
            & ((inner >> b_k) == i)
            & ((inner & (kr - 1)) == (old & (kr - 1)))
        )
    new, old = iota((LANES, LANES), 0), iota((LANES, LANES), 1)
    b_r = log2(rw)
    zc = LANES // (CORES * rw)
    o_r = old & (rw - 1)
    o_c = (old >> b_r) & (CORES - 1)
    o_z = old >> (b_r + b_c)
    perm_w[...] = one_hot(new == (o_c * zc + o_z) * rw + o_r)

    wait_recv(min_a.at[pl.ds(0, nz - 1)], recv.at[0])
    for i in range(nz):
        m2d[i : i + 1, :] = min_a[i]
    min_b[p] = m2d[...]

    def send_mb(k):
        _, dev = p_peer(k)
        push(m2d, min_b.at[p], send.at[4], recv.at[3], (dev, x))

    loop(1, np_, send_mb)

    def forward(i):
        wait_recv(in_a.at[i, pl.ds(0, nz - 1)], recv_a.at[i])
        if i + AHEAD < ch:
            send_a(i + AHEAD)
        moved = dot(perm_b[...], in_a[i].reshape(places, LANES)).astype(BF16)
        out_b[i] = moved.reshape(np_, nz * cap, LANES)
        in_b[i, p] = out_b[i, p]

        for k in sorted(range(1, np_), key=lambda k: abs(k - np_ // 2)):
            pp, dev = p_peer(k)
            push(out_b.at[i, pp], in_b.at[i, p], send.at[5], recv_b.at[i], (dev, x))

    forward(0)

    wait_recv(min_b.at[pl.ds(0, np_ - 1)], recv.at[3])
    pick = one_hot(
        iota((lanes_m, places), 0) == p * cap + (iota((lanes_m, places), 1) & (cap - 1))
    )
    table = dot(min_b[...].reshape(np_ * nz, lanes_m).astype(BF16), pick)
    slot_row = jnp.sum(
        jnp.where(
            iota((np_ * nz, places), 0) == (iota((np_ * nz, places), 1) >> log2(cap)), table, 0.0
        ),
        axis=0,
        keepdims=True,
    )
    land = one_hot(iota((tok, places), 0).astype(F32) == slot_row)
    gate = gate_ref[:, pl.ds(pl.multiple_of(x * dx, LANES), dx)]

    def landing(i):
        wait_recv(in_b.at[i, pl.ds(0, np_ - 1)], recv_b.at[i])
        grad_out = dot(land, in_b[i].reshape(places, LANES)).astype(BF16)
        bgx[i, x] = (gate[:, i * LANES : (i + 1) * LANES] * grad_out.astype(F32)).astype(BF16)

        for k in sorted(range(1, nx), key=lambda k: abs(k - nx // 2)):
            xx = lax.rem(x + k, nx)
            push(bgx.at[i, x], bgx.at[i, x], send.at[6], recv_x.at[i], (d, xx))

    def project(i):
        wait_recv(bgx.at[i, pl.ds(0, nx - 1)], recv_x.at[i])
        part = ga_acc[...] if i else None
        for xx in range(nx):
            first = xx * dx + i * LANES
            term = dot(bgx[i, xx], w_ref[:, first : first + LANES], NT)
            part = term if part is None else part + term
        ga_acc[...] = part

    def turn(i):
        bgt[i] = dot(perm_w[...], bgx[i, x], NT).astype(BF16).reshape(CORES, zc * rw, tok)
        push(bgt.at[i, 1 - c], bgt_in.at[i], send.at[7], recv_t.at[i], (twin, x))

    def outer(i):
        wait_recv(bgt_in.at[i], recv_t.at[i])
        for yy in range(ny):
            part = dot(bgt[i, c], aall[yy]) + dot(bgt_in[i], asib[yy])
            wo_out[i, yy] = part.astype(BF16).reshape(zc, rw, hw)
        wo_in[i, y] = wo_out[i, y]

        def step(k):
            yy, dev = y_peer(k)
            push(wo_out.at[i, yy], wo_in.at[i, y], send.at[8], recv_w.at[i], (dev, x))

        loop(1, ny, step)

    landing(0)
    turn(0)

    wait_recv(aall.at[pl.ds(0, nx - 1)], recv.at[2])
    push(aall, asib, send.at[2], recv.at[1], (twin, x))

    for i in range(1, ch):
        forward(i)
        if i == 1:
            wait_recv(asib, recv.at[1])
        outer(i - 1)
        project(i - 1)
        landing(i)
        turn(i)

    outer(ch - 1)

    def sum_wo(i):
        wait_recv(wo_in.at[i, pl.ds(0, ny - 1)], recv_w.at[i])
        for k in range(zc):
            zz = i * zc + k
            acc = wo_in[i, 0, k].astype(F32)
            for j in range(1, ny):
                acc = acc + wo_in[i, j, k].astype(F32)
            wz_out[zz] = acc.astype(BF16)

            @pl.when(z != zz)
            def _():
                dev = (y * nz + zz) * CORES + c
                push(wz_out.at[zz], wz_in.at[z], send.at[11], recv.at[7], (dev, x))

            @pl.when(z == zz)
            def _():
                wz_in[z] = wz_out[zz]

    for i in range(ch - 1):
        sum_wo(i)
    project(ch - 1)
    ga = ga_acc[...].astype(BF16)
    score_grads = []
    for h in range(heads):
        cols = slice(h * HD, (h + 1) * HD)
        ga_h = ga[:, cols]
        gp = dot(vp[:, cols], ga_h, NT)
        w = wts[h]
        delta = jnp.sum(w * gp, axis=0, keepdims=True)
        sg = (w * (gp - delta)).astype(BF16)
        score_grads.append(sg)
        gk_h = (scale * dot(sg, q_ref[:, cols])).astype(BF16)
        gv_h = dot(probs[h], ga_h).astype(BF16)
        kc_out[h, :, 0] = gk_h.reshape(CORES, ny, nz * kr, HD)
        kc_out[h, :, 1] = gv_h.reshape(CORES, ny, nz * kr, HD)
        push(kc_out.at[h, 1 - c], kc_in.at[h], send.at[9], recv_c.at[h], (twin, x))

    sum_wo(ch - 1)

    for h in range(heads):
        wait_recv(kc_in.at[h], recv_c.at[h])
        for yy in range(ny):
            for j in range(2):
                ky_out[h, yy, j] = (
                    kc_out[h, c, j, yy].astype(F32) + kc_in[h, j, yy].astype(F32)
                ).astype(BF16)
        ky_in[h, y] = ky_out[h, y]

        for k in sorted(range(1, ny), key=lambda k: abs(k - ny // 2)):
            yy, dev = y_peer(k)
            push(ky_out.at[h, yy], ky_in.at[h, y], send.at[10], recv_y.at[h], (dev, x))

    acc = None
    for h in range(heads):
        wait_recv(ky_in.at[h, pl.ds(0, ny - 1)], recv_y.at[h])
        for j in range(2):
            tot = ky_in[h, 0, j].astype(F32)
            for i in range(1, ny):
                tot = tot + ky_in[h, i, j].astype(F32)
            part = dot(perm_k[j * halves + h], tot.astype(BF16))
            acc = part if acc is None else acc + part
    kz_out[...] = acc.astype(BF16).reshape(nz, rows, LANES)
    kz_in[z] = kz_out[z]

    def send_kz(k):
        zz, dev = z_peer(k)
        push(kz_out.at[zz], kz_in.at[z], send.at[12], recv.at[8], (dev, x))

    far_first(send_kz)

    wait_recv(wz_in.at[pl.ds(0, nz - 1)], recv.at[7])
    acc = wz_in[0].astype(F32)
    for i in range(1, nz):
        acc = acc + wz_in[i].astype(F32)
    wf_out[...] = acc

    @pl.when(x != y)
    def _():
        push(wf_out, wf_in, send.at[13], recv.at[6], mirror)

    @pl.when(x == y)
    def _():
        wf_in[...] = wf_out[...]

    for h in range(heads):
        cols = slice(h * HD, (h + 1) * HD)
        gq_ref[:, cols] = (scale * dot(score_grads[h], kp[:, cols], TN)).astype(BF16)

    wait_recv(kz_in.at[pl.ds(0, nz - 1)], recv.at[8])
    acc = kz_in[0].astype(F32)
    for i in range(1, nz):
        acc = acc + kz_in[i].astype(F32)
    for h in range(halves):
        cols = slice(h * LANES, (h + 1) * LANES)
        gk_ref[:, cols] = acc[h * kr : (h + 1) * kr, :]
        gv_ref[:, cols] = acc[(halves + h) * kr : (halves + h + 1) * kr, :]

    @pl.when(x != y)
    def _():
        wait_recv(wf_in, recv.at[6])

    gwo_ref[...] = wf_in[...]

    wait_send(mout_a.at[pl.ds(0, nz - 1)], send.at[0])
    wait_send(out_a.at[:, pl.ds(0, nz - 1)], send.at[1])
    wait_send(aall, send.at[2])
    wait_send(aall.at[pl.ds(0, nx - 1)], send.at[3])
    wait_send(min_b.at[pl.ds(0, np_ - 1)], send.at[4])
    wait_send(out_b.at[:, pl.ds(0, np_ - 1)], send.at[5])
    wait_send(bgx.at[:, pl.ds(0, nx - 1)], send.at[6])
    wait_send(bgt_in, send.at[7])
    wait_send(wo_out.at[:, pl.ds(0, ny - 1)], send.at[8])
    wait_send(kc_in, send.at[9])
    wait_send(ky_out.at[:, pl.ds(0, ny - 1)], send.at[10])

    wait_send(wz_out.at[pl.ds(0, nz - 1)], send.at[11])

    @pl.when(x != y)
    def _():
        wait_send(wf_out, send.at[13])

    wait_send(kz_out.at[pl.ds(0, nz - 1)], send.at[12])


def store(*refs):
    count = (len(refs) - 1) // 2
    done = refs[-1]
    copies = [
        pltpu.make_async_copy(refs[i], refs[count + i], done.at[i]) for i in range(count)
    ]
    for copy in copies:
        copy.start()
    for copy in copies:
        copy.wait()


def body(face_grads, face_owner, face_slot, queries, keys, values, w_out, branch_gate):
    nx = lax.axis_size("tensor")
    dp = lax.axis_size("dp")
    ny = nx
    nz = dp // (ny * CORES)
    np_ = ny * CORES
    faces, dx = face_grads.shape
    tok, hw = queries.shape
    ctx = keys.shape[0]
    heads = hw // HD
    cap = 2 * faces // dp
    ch = dx // LANES
    ma = np_ * cap
    places = nz * ma
    width = w_out.shape[1]
    rw = width // dp
    kr = ctx // dp
    rows = 2 * (hw // LANES) * kr
    lanes_m = max(LANES, ma)
    vmem = pltpu.VMEM
    dma = pltpu.SemaphoreType.DMA
    spec = pl.BlockSpec(memory_space=pltpu.VMEM)
    outs = (
        jax.ShapeDtypeStruct((tok, hw), BF16),
        jax.ShapeDtypeStruct((rw, hw), F32),
        jax.ShapeDtypeStruct((kr, hw), F32),
        jax.ShapeDtypeStruct((kr, hw), F32),
    )
    results = pl.pallas_call(
        functools.partial(kernel, nx, nz),
        out_shape=outs,
        in_specs=[pl.BlockSpec(memory_space=pltpu.HBM)] * 8,
        out_specs=(spec,) * 4,
        scratch_shapes=[
            vmem((ch, nz, ma, LANES), BF16),
            vmem((ch, nz, ma, LANES), BF16),
            vmem((nz, 1, lanes_m), F32),
            vmem((nz, 1, lanes_m), F32),
            vmem((nz, lanes_m), F32),
            vmem((np_, nz, lanes_m), F32),
            vmem((ch, np_, nz * cap, LANES), BF16),
            vmem((ch, np_, nz * cap, LANES), BF16),
            vmem((nx, tok, hw), BF16),
            vmem((nx, tok, hw), BF16),
            vmem((ch, nx, tok, LANES), BF16),
            vmem((ch, CORES, LANES // CORES, tok), BF16),
            vmem((ch, LANES // CORES, tok), BF16),
            vmem((ch, ny, nz // ch, rw, hw), BF16),
            vmem((ch, ny, nz // ch, rw, hw), BF16),
            vmem((nz, rw, hw), BF16),
            vmem((nz, rw, hw), BF16),
            vmem((rw, hw), F32),
            vmem((rw, hw), F32),
            vmem((heads, CORES, 2, ny, nz * kr, HD), BF16),
            vmem((heads, 2, ny, nz * kr, HD), BF16),
            vmem((heads, ny, 2, nz * kr, HD), BF16),
            vmem((heads, ny, 2, nz * kr, HD), BF16),
            vmem((nz, rows, LANES), BF16),
            vmem((nz, rows, LANES), BF16),
            vmem((heads, ctx, tok), F32),
            vmem((heads, ctx, tok), BF16),
            vmem((ctx, hw), BF16),
            vmem((ctx, hw), BF16),
            vmem((tok, hw), F32),
            vmem((places, places), BF16),
            vmem((LANES, LANES), BF16),
            vmem((2 * (hw // LANES), nz * rows, nz * kr), BF16),
            vmem((hw, width), BF16),
            vmem((faces, dx), BF16),
            vmem((1, faces), jnp.int32),
            vmem((1, faces), jnp.int32),
            vmem((tok, hw), BF16),
            vmem((ctx, hw), BF16),
            vmem((ctx, hw), BF16),
            vmem((1, width), F32),
            dma((8,)),
            dma((14,)),
            dma((ch,)),
            dma((ch,)),
            dma((ch,)),
            dma((ch,)),
            dma((ch,)),
            dma((heads,)),
            dma((heads,)),
            dma((10,)),
        ],
        compiler_params=pltpu.CompilerParams(
            collective_id=0, has_side_effects=True, vmem_limit_bytes=24 << 20
        ),
    )(
        *[
            pltpu.with_memory_space_constraint(a, pltpu.HBM)
            for a in (
                face_grads,
                face_owner.reshape(1, faces),
                face_slot.reshape(1, faces),
                queries,
                keys,
                values,
                w_out,
                branch_gate.reshape(1, width),
            )
        ]
    )
    return pl.pallas_call(
        store,
        out_shape=outs,
        in_specs=[spec] * 4,
        out_specs=(pl.BlockSpec(memory_space=pltpu.HBM),) * 4,
        scratch_shapes=[dma((4,))],
    )(*[pltpu.with_memory_space_constraint(r, pltpu.VMEM) for r in results])


def solution(mesh):
    in_specs = (
        P("dp", "tensor"),
        P("dp", None),
        P("dp", None),
        P("dp", "tensor"),
        P(None, "tensor"),
        P(None, "tensor"),
        P("tensor", None),
        P(),
    )
    out_specs = (P("dp", "tensor"), P("dp", "tensor"), P("dp", "tensor"), P("dp", "tensor"))
    return jax.shard_map(body, mesh=mesh, in_specs=in_specs, out_specs=out_specs, check_vma=False)
```
